512 devices in a mesh: ex: 8 (over z), tp: 16 (over y_lo, x, core), blk: 4 (over y_hi).
Axes of the slice: x: 4, y: 8 (y_hi: 4, y_lo: 2; y = y_hi * 2 + y_lo), z: 8, core: 2. Of those that a mesh axis runs over, the one named last changes fastest.
Arguments:
- gradients: bfloat16 [2048, 32768], P('ex', 'tp'), may hold values from -6 to 6
- selection: int32 [1024], P('ex'), may hold values from 0 to 255, as said below
- seed_value: int32 [1], replicated, may hold values from 0 to 999999999
- ridge_value: float32 [1], replicated, may hold values from 0.3 to 3
Outputs:
- panel_out: float32 [8192, 512], P(('ex', 'blk'))
- trailing: float32 [8192, 8192], P(('ex', 'blk'), 'tp')
The draws below stay inside these ranges and needn't reach their ends.
Inputs may be any that keep to these rules, and one draw needn't show every extreme that they name: `selection`: within each aligned block of 128 entries the values are distinct, and 0 and 255 occur in every block.
All inputs are finite; a program needn't handle non-finite values.
Results may differ from the reference program's by a relative error of at most 0.0046.
Values may be sent and summed in bfloat16 or wider, within the bound.
A program may use at most 64 MiB of HBM per device.

```python
import math
import jax
import jax.numpy as jnp
from jax import lax

PANEL = 512
K = 8192
E_DEV = 128
GL = 2048
POOL_DEV = 256
POOLS = 2048
EXAMPLES = 1024
GDIM = 32768


def draw_selection(key, part):
    block_count = EXAMPLES // E_DEV

    def one_block(block_key):
        first_key, second_key = jax.random.split(block_key)
        middle = jax.random.permutation(first_key, POOL_DEV - 2).astype(jnp.int32) + 1
        picked = jnp.concatenate([jnp.zeros((1,), jnp.int32), jnp.full((1,), POOL_DEV - 1, jnp.int32), middle[:E_DEV - 2]])
        return jax.random.permutation(second_key, picked)
    keys = jax.random.split(jax.random.fold_in(key, 7), block_count)
    return jax.vmap(one_block)(keys).reshape(-1).astype(jnp.int32)


def shard_levels(key, shape, shards, smallest, largest):
    gain = 1.0
    for position, parts in shards:
        steps = jax.random.uniform(jax.random.fold_in(jax.random.fold_in(key, 6), position), (parts,), jnp.float32, smallest / len(shards), largest / len(shards))
        gain = gain * jnp.repeat(jnp.exp(steps), shape[position] // parts).reshape((-1,) + (1,) * (len(shape) - 1 - position))
    return gain


def normal_values(stream_key, extent, spread, bound, cuts=(), held_as=jnp.bfloat16):
    entries = spread * jax.random.normal(stream_key, extent, jnp.float32)
    if cuts:
        entries = entries * shard_levels(stream_key, extent, cuts, -0.22, 0.18)
    return jnp.clip(entries, -bound, bound).astype(held_as)


def setup_inputs(seed: int = 0) -> dict:
    splits = jax.random.split(jax.random.key(seed), 5)
    gradients = normal_values(splits[0], (POOLS, GDIM), 1.0, 6.0, ((0, 8), (1, 16)))
    selection = draw_selection(jax.random.fold_in(splits[4], 71), 0)
    seed_value = jax.random.randint(splits[2], (1,), 0, 1000000000).astype(jnp.int32)
    ridge_value = jnp.clip(jnp.exp(jax.random.uniform(splits[3], (1,), jnp.float32, math.log(0.3), math.log(3.0))), 0.3, 3.0)
    return {"gradients": gradients, "selection": selection, "seed_value": seed_value, "ridge_value": ridge_value}


def scramble(hashed, amount):
    return hashed ^ lax.shift_right_logical(hashed, jnp.full_like(hashed, amount))

def sign_block(seed_word, coordinates, features):
    hashed = coordinates[:, None] * jnp.int32(-1640531535) + features[None, :] * jnp.int32(668265263) + seed_word
    hashed = scramble(hashed, 16) * jnp.int32(-2048144789)
    hashed = scramble(hashed, 13) * jnp.int32(-1028477387)
    hashed = scramble(hashed, 16)
    bit_value = lax.shift_right_logical(hashed, jnp.full_like(hashed, 7)) & jnp.int32(1)
    return jnp.int32(1) - jnp.int32(2) * bit_value

def reference(gradients, selection, seed_value, ridge_value):
    row_ids = selection + jnp.arange(EXAMPLES, dtype=jnp.int32) // E_DEV * POOL_DEV
    chosen = gradients[row_ids].astype(jnp.float32)
    stride = min(512, GL)
    feature_ids = jnp.arange(K, dtype=jnp.int32)

    def accumulate(running, index):
        coordinates = index * stride + jnp.arange(stride, dtype=jnp.int32)
        sign_values = sign_block(seed_value[0], coordinates, feature_ids).astype(jnp.float32)
        slab = lax.dynamic_slice_in_dim(chosen, index * stride, stride, 1)
        return (running + jnp.dot(slab, sign_values, precision=lax.Precision.HIGHEST), None)
    projected, _ = lax.scan(accumulate, jnp.zeros((EXAMPLES, K), jnp.float32), jnp.arange(GDIM // stride, dtype=jnp.int32))
    scaling = 1.0 / math.sqrt(GDIM)
    features = (projected * scaling).astype(jnp.bfloat16).astype(jnp.float32)
    gram = jnp.dot(features.T, features, precision=lax.Precision.HIGHEST) / float(EXAMPLES)
    diagonal_ids = jnp.arange(K, dtype=jnp.int32)
    gram = gram.at[diagonal_ids, diagonal_ids].add(ridge_value[0])
    factor = jnp.linalg.cholesky(gram[:PANEL, :PANEL])
    lifted = jax.scipy.linalg.solve_triangular(factor, gram[:PANEL, :], lower=True)
    panel_out = lifted.T
    trailing = gram - jnp.dot(panel_out, lifted, precision=lax.Precision.HIGHEST)
    return (panel_out, trailing)
```

```python
import math

import jax
import jax.numpy as jnp
from jax import lax
from jax.experimental import pallas as pl
from jax.experimental.pallas import tpu as pltpu
from jax.sharding import PartitionSpec as P

SB = 128
EX, TP, BLK = 8, 16, 4
CHIPS = TP // 2
K, GDIM, EXAMPLES, PANEL = 8192, 32768, 1024, 512
HI = lax.Precision.HIGHEST
NT = (((1,), (1,)), ((), ()))
TN = (((0,), (0,)), ((), ()))
NN = (((1,), (0,)), ((), ()))


def wrap(value):
    value &= 0xFFFFFFFF
    return value - (1 << 32) if value >= (1 << 31) else value


C1, C2, C3 = -1640531535, 668265263, -2048144789
C4 = wrap(-1028477387 << 8)


def slot_of(b):
    return 2 * (b % 2) + b // 2


def right_shift(value, amount):
    return lax.shift_right_logical(value, jnp.full_like(value, amount))


def project_kernel(seed_ref, grads_ref, sel_ref, out_ref, chosen_ref, cvec_ref, sign_ref):
    block = pl.program_id(0)
    pool, coords = grads_ref.shape

    @pl.when(block == 0)
    def _():
        hot = (lax.broadcasted_iota(jnp.int32, (pool, SB), 0) == sel_ref[...]).astype(jnp.float32)
        hot = hot.astype(jnp.bfloat16)
        for s in range(coords // 256):
            chosen_ref[pl.ds(s * 256, 256), :] = lax.dot_general(
                grads_ref[:, s * 256 : (s + 1) * 256], hot, TN, preferred_element_type=jnp.float32
            ).astype(jnp.bfloat16)
        first_coord = lax.axis_index("tp") * coords
        cvec_ref[...] = (first_coord + lax.broadcasted_iota(jnp.int32, (8, coords), 1)) * jnp.int32(
            C1
        ) + seed_ref[0]

    first = block * PANEL + slot_of(lax.axis_index("blk")) * SB

    def rows(r, carry):
        ids = first + r * 16 + lax.broadcasted_iota(jnp.int32, (8, 128), 0)
        low = ids * jnp.int32(C2)
        high = low + jnp.int32(wrap(8 * C2))
        start = pl.multiple_of(r * 16, 16)
        for s in range(coords // 128):
            c = cvec_ref[:, s * 128 : (s + 1) * 128]
            halves = []
            for f in (low, high):
                h = c + f
                h = (h ^ right_shift(h, 16)) * jnp.int32(C3)
                h = (h ^ right_shift(h, 13)) * jnp.int32(C4)
                h = h ^ (h << 16)
                halves.append(jnp.where(h < 0, jnp.float32(-1), jnp.float32(1)))
            sign_ref[pl.ds(start, 16), s * 128 : (s + 1) * 128] = jnp.concatenate(halves, axis=0).astype(
                jnp.bfloat16
            )
        return carry

    lax.fori_loop(0, SB // 16, rows, 0)
    out_ref[0] = jnp.dot(sign_ref[...], chosen_ref[...], preferred_element_type=jnp.float32).astype(out_ref.dtype)


def project(seed, grads, sel):
    pool, coords = grads.shape
    return pl.pallas_call(
        project_kernel,
        grid=(TP,),
        out_shape=jax.ShapeDtypeStruct((TP, SB, SB), jnp.bfloat16),
        in_specs=[
            pl.BlockSpec(memory_space=pltpu.SMEM),
            pl.BlockSpec(grads.shape, lambda i: (0, 0)),
            pl.BlockSpec((1, SB), lambda i: (0, 0)),
        ],
        out_specs=pl.BlockSpec((1, SB, SB), lambda i: (i, 0, 0)),
        scratch_shapes=[
            pltpu.VMEM((coords, SB), jnp.bfloat16),
            pltpu.VMEM((8, coords), jnp.int32),
            pltpu.VMEM((SB, coords), jnp.bfloat16),
        ],
        name="project",
    )(seed, grads, sel)


def exchange_kernel(
    parts, fp, fr, fc, prx, rx,
    ps, pr, ms, mr, pys, pyr, mys, myr, rps, rpr, pzs, pzr,
    rs_, rr_, ls_, lr_, ras, rar, rds, rdr, pas, par, pds, pdr, loc,
):
    z, t, b = lax.axis_index("ex"), lax.axis_index("tp"), lax.axis_index("blk")
    u, c = t // 2, t % 2
    slot = slot_of(b)
    scaling = jnp.float32(1.0 / math.sqrt(GDIM))
    pending = []

    def to(**axes):
        at = {"ex": z, "tp": t, "blk": b}
        at.update(axes)
        return (at["ex"], at["tp"], at["blk"])

    def copy(src, dst, send, recv, target):
        return pltpu.make_async_remote_copy(
            src_ref=src, dst_ref=dst, send_sem=send, recv_sem=recv,
            device_id=target, device_id_type=pl.DeviceIdType.MESH,
        )

    def go(src, dst, send, recv, target):
        one = copy(src, dst, send, recv, target)
        one.start()
        pending.append(one)
        return one

    def lanes(index):
        return pl.ds(pl.multiple_of(index * SB, SB), SB)

    tp_peers = [(d, lax.rem(t + d, TP)) for d in range(1, TP)]
    chip_peers = [(d, lax.rem(u + d, CHIPS) * 2 + c) for d in range(1, CHIPS)]
    blk_peers = [(d, lax.rem(b + d, BLK)) for d in range(1, BLK)]
    ex_peers = [(d, lax.rem(z + d, EX)) for d in range(1, EX)]
    other = u * 2 + 1 - c
    mate = to(ex=u, tp=2 * z + b // 2, blk=2 * c + b % 2)
    alone = jnp.logical_and(u == z, b // 2 == c)

    barrier = pltpu.get_barrier_semaphore()

    def greet(target):
        pl.semaphore_signal(barrier, inc=1, device_id=target, device_id_type=pl.DeviceIdType.MESH)

    for _, p in tp_peers:
        greet(to(tp=p))
    for _, p in blk_peers:
        greet(to(blk=p))
    for _, p in ex_peers:
        greet(to(ex=p))

    @pl.when(jnp.logical_not(alone))
    def _():
        greet(mate)

    greeted = len(tp_peers) + len(blk_peers) + len(ex_peers) + 1
    pl.semaphore_wait(barrier, greeted - alone.astype(jnp.int32))

    panel_in, main_in = [], []
    for d, p in tp_peers:
        rows = pl.ds(pl.multiple_of((p // 2) * 16, 16), 16)
        panel_in.append(go(parts.at[0, rows, :], prx.at[d], ps.at[d], pr.at[d], to(tp=p)))
    for d, p in tp_peers:
        main_in.append(go(parts.at[p], rx.at[d], ms.at[d], mr.at[d], to(tp=p)))
    for one in panel_in:
        one.wait_recv()
    total = parts[0, pl.ds(pl.multiple_of(u * 16, 16), 16), :].astype(jnp.float32)
    for d in range(1, TP):
        total = total + prx[d].astype(jnp.float32)
    fp[slot, u, :, lanes(z)] = (total * scaling).astype(jnp.bfloat16)
    mine = fp.at[slot, u, :, lanes(z)]
    panel_y = [go(mine, mine, pys.at[d], pyr.at[d], to(blk=p)) for d, p in blk_peers]

    for one in main_in:
        one.wait_recv()
    total = parts[t].astype(jnp.float32)
    for d in range(1, TP):
        total = total + rx[d].astype(jnp.float32)
    fc[lanes(slot), lanes(z)] = (total * scaling).astype(jnp.bfloat16)
    mine = fc.at[lanes(slot), lanes(z)]
    main_y = [None] + [go(mine, mine, mys.at[d], myr.at[d], to(blk=p)) for d, p in blk_peers]

    row_slot = fr.at[lanes(b // 2), lanes(z)]
    moved = copy(mine, row_slot, rps, rpr, mate)

    @pl.when(alone)
    def _():
        pltpu.make_async_copy(mine, row_slot, loc).start()

    @pl.when(jnp.logical_not(alone))
    def _():
        moved.start()

    right, left = to(ex=lax.rem(z + 1, EX)), to(ex=lax.rem(z + EX - 1, EX))
    rights, lefts = {}, {}

    def piece(step, j):
        row = slot_of(lax.rem(b + BLK - j, BLK))
        return fc.at[lanes(row), lanes(lax.rem(z + step + EX, EX))]

    def pass_right(s, j):
        at = piece(-s, j)
        rights[s, j] = go(at, at, rs_.at[s, j], rr_.at[s, j], right)

    def pass_left(s, j):
        at = piece(s, j)
        lefts[s, j] = go(at, at, ls_.at[s, j], lr_.at[s, j], left)

    for j in range(BLK):
        if j:
            main_y[j].wait_recv()
        pass_right(0, j)
        pass_left(0, j)

    for one in panel_y:
        one.wait_recv()
    mine = fp.at[:, u, :, lanes(z)]
    panel_z = [go(mine, mine, pzs.at[d], pzr.at[d], to(ex=p)) for d, p in ex_peers]

    @pl.when(alone)
    def _():
        pltpu.make_async_copy(piece(0, 0), row_slot, loc).wait()

    @pl.when(jnp.logical_not(alone))
    def _():
        moved.wait_send()
        moved.wait_recv()

    def row_at(chip):
        return fr.at[lanes(c), lanes(chip)]

    mine = row_at(u)
    rows_in = [go(mine, mine, ras.at[d], rar.at[d], to(tp=p)) for d, p in chip_peers]
    rows_over = [go(mine, mine, rds.at[0], rdr.at[0], to(tp=other))]

    for one in panel_z:
        one.wait_recv()

    def panel_at(chip):
        return fp.at[pl.ds(2 * c, 2), chip]

    mine = panel_at(u)
    panel_a = [go(mine, mine, pas.at[d], par.at[d], to(tp=p)) for d, p in chip_peers]

    for s in range(1, EX // 2):
        for j in range(BLK):
            rights[s - 1, j].wait_recv()
            if s < EX // 2 - 1 or j < BLK // 2:
                pass_right(s, j)
            lefts[s - 1, j].wait_recv()
            if s < EX // 2 - 1 or j >= BLK // 2:
                pass_left(s, j)

    for d in range(1, CHIPS):
        rows_in[d - 1].wait_recv()
        at = row_at(lax.rem(u + CHIPS - d, CHIPS))
        rows_over.append(go(at, at, rds.at[d], rdr.at[d], to(tp=other)))
    panel_over = []
    for d in range(1, CHIPS):
        panel_a[d - 1].wait_recv()
        at = panel_at(lax.rem(u + CHIPS - d, CHIPS))
        panel_over.append(go(at, at, pds.at[d], pdr.at[d], to(tp=other)))
    last = EX // 2 - 1
    for j in range(BLK // 2):
        rights[last, j].wait_recv()
        lefts[last, BLK // 2 + j].wait_recv()
    for one in rows_over + panel_over:
        one.wait_recv()
    for one in pending:
        one.wait_send()


def exchange(parts):
    bf = jnp.bfloat16
    dma = pltpu.SemaphoreType.DMA
    sems = []
    for n in (TP, TP, BLK, BLK):
        sems += [dma((n,)), dma((n,))]
    sems += [dma, dma, dma((EX,)), dma((EX,))]
    sems += [dma((EX // 2, BLK))] * 4
    sems += [dma((CHIPS,))] * 8
    sems += [dma]
    vmem = pl.BlockSpec(memory_space=pltpu.VMEM)
    return pl.pallas_call(
        exchange_kernel,
        out_shape=(
            jax.ShapeDtypeStruct((BLK, CHIPS, 16, EXAMPLES), bf),
            jax.ShapeDtypeStruct((2 * SB, EXAMPLES), bf),
            jax.ShapeDtypeStruct((PANEL, EXAMPLES), bf),
        ),
        in_specs=[vmem],
        out_specs=(vmem, vmem, vmem),
        scratch_shapes=[pltpu.VMEM((TP, 16, SB), bf), pltpu.VMEM((TP, SB, SB), bf)] + sems,
        compiler_params=pltpu.CompilerParams(collective_id=0, has_side_effects=True),
        name="exchange",
    )(parts)


def split3(x):
    a = x.astype(jnp.bfloat16)
    r = x - a.astype(jnp.float32)
    b = r.astype(jnp.bfloat16)
    c = (r - b.astype(jnp.float32)).astype(jnp.bfloat16)
    return a, b, c

def dot3(x, y, dims):
    xa, xb, xc = split3(x)
    ya, yb, yc = split3(y)
    kx, ky = dims[0][0][0], dims[0][1][0]
    left = jnp.concatenate([xa, xa, xb, xa, xb, xc], axis=kx)
    right = jnp.concatenate([ya, yb, ya, yc, yb, ya], axis=ky)
    return lax.dot_general(left, right, dims, preferred_element_type=jnp.float32)

def base_inverse(s):
    n = 128
    rowid = lax.broadcasted_iota(jnp.int32, (8, 128), 0)
    lane = lax.broadcasted_iota(jnp.int32, (8, 128), 1)
    top = [s[8 * i:8 * i + 8, :] for i in range(n // 8)]
    aug = [(lane == rowid + 8 * i).astype(jnp.float32) for i in range(n // 8)]
    done = []
    for m in range(n // 8):
        r, a = top[m], aug[m]
        v = [jnp.broadcast_to(r[:, 8 * m + k:8 * m + k + 1], (8, 128)) for k in range(8)]
        scale = jnp.zeros((8, 128), jnp.float32)
        for j in range(8):
            d = jnp.broadcast_to(v[j][j:j + 1, :], (8, 128))
            scale = jnp.where(rowid == j, lax.rsqrt(d), scale)
            if j < 7:
                f = jnp.where(rowid > j, v[j] / d, 0.0)
                for k in range(j + 1, 8):
                    v[k] = v[k] - f * jnp.broadcast_to(v[k][j:j + 1, :], (8, 128))
                r = r - f * jnp.broadcast_to(r[j:j + 1, :], (8, 128))
                a = a - f * jnp.broadcast_to(a[j:j + 1, :], (8, 128))
        r = r * scale
        a = a * scale
        done.append(a)
        if m < n // 8 - 1:
            ra, rb, rc = split3(r)
            aa, ab, ac = split3(a)
            lo = 8 * (m + 1)
            left = jnp.concatenate([ra, ra, rb, ra, rb, rc], axis=0)
            right = jnp.concatenate([jnp.concatenate([x, y], axis=1) for x, y in
                                     ((ra, aa), (rb, ab), (ra, aa), (rc, ac), (rb, ab), (ra, aa))], axis=0)
            u = lax.dot_general(left, right, TN, preferred_element_type=jnp.float32)
            for i in range(m + 1, n // 8):
                top[i] = top[i] - u[8 * i:8 * i + 8, :128]
                aug[i] = aug[i] - u[8 * i:8 * i + 8, 128:]
    return jnp.concatenate(done, axis=0)

def factor_inverse(A, N, M):
    for k in range(4):
        rk = slice(128 * k, 128 * k + 128)
        w = base_inverse(A[rk, rk])
        if k > 0:
            M[rk, :128 * k] = dot3(w, N[rk, :128 * k], (((1,), (0,)), ((), ())))
        M[rk, rk] = w
        if k < 3:
            M[rk, 128 * (k + 1):] = jnp.zeros((128, 512 - 128 * (k + 1)), jnp.float32)
            y = dot3(w, A[rk, 128 * (k + 1):], (((1,), (0,)), ((), ())))
            ym = M[rk, :128 * (k + 1)]
            for i in range(k + 1, 4):
                ri = slice(128 * i, 128 * i + 128)
                yi = y[:, 128 * (i - k - 1):128 * (i - k)]
                A[ri, 128 * i:] = A[ri, 128 * i:] - dot3(yi, y[:, 128 * (i - k - 1):], TN)
                up = dot3(yi, ym, TN)
                if k > 0:
                    N[ri, :128 * k] = N[ri, :128 * k] - up[:, :128 * k]
                N[ri, rk] = -up[:, 128 * k:]

def final_kernel(ridge, fp, fr, fc, pan, trail, A, N, M, X):
    inv = jnp.float32(1.0 / fp.shape[1])
    g, t = lax.axis_index("ex") * BLK + lax.axis_index("blk"), lax.axis_index("tp")
    rv = ridge[0]
    def diag(shape, r0, c0):
        return jnp.where(lax.broadcasted_iota(jnp.int32, shape, 0) + r0 == lax.broadcasted_iota(jnp.int32, shape, 1) + c0, rv, 0.0)
    A[...] = lax.dot_general(fp[...], fp[...], NT, preferred_element_type=jnp.float32) * inv + diag((512, 512), 0, 0)
    factor_inverse(A, N, M)
    A[...] = lax.dot_general(fp[...], fc[...], NT, preferred_element_type=jnp.float32) * inv + diag((512, 512), 0, t * 512)
    X[...] = jnp.dot(M[...], A[...], precision=HI)
    N[:256] = lax.dot_general(fr[...], fp[...], NT, preferred_element_type=jnp.float32) * inv + diag((256, 512), g * 256, 0)
    pan[...] = lax.dot_general(N[:256], M[...], NT, precision=HI)
    own = lax.dot_general(fr[...], fc[...], NT, preferred_element_type=jnp.float32) * inv + diag((256, 512), g * 256, t * 512)
    trail[...] = own - jnp.dot(pan[...], X[...], precision=HI)

def finish(ridge, fp, fr, fc):
    return pl.pallas_call(
        final_kernel,
        out_shape=(jax.ShapeDtypeStruct((256, 512), jnp.float32), jax.ShapeDtypeStruct((256, 512), jnp.float32)),
        in_specs=[pl.BlockSpec(memory_space=pltpu.SMEM)] + [pl.BlockSpec(memory_space=pltpu.VMEM)] * 3,
        out_specs=(pl.BlockSpec(memory_space=pltpu.VMEM),) * 2,
        scratch_shapes=[pltpu.VMEM((512, 512), jnp.float32)] * 4,
        name="finish",
    )(ridge, fp, fr, fc)


def shards(gradients, selection, seed_value, ridge_value):
    parts = project(seed_value, gradients, selection.reshape(1, SB))
    fp, fr, fc = exchange(parts)
    return finish(ridge_value, fp.reshape(PANEL, EXAMPLES), fr, fc)


def solution(mesh):
    in_specs = (P("ex", "tp"), P("ex"), P(), P())
    out_specs = (P(("ex", "blk"), None), P(("ex", "blk"), "tp"))
    return jax.shard_map(shards, mesh=mesh, in_specs=in_specs, out_specs=out_specs, check_vma=False)
```

```python
import math

import jax
import jax.numpy as jnp
from jax import lax
from jax.experimental import pallas as pl
from jax.experimental.pallas import tpu as pltpu
from jax.sharding import PartitionSpec as P

SB = 128
EX, TP, BLK = 8, 16, 4
CHIPS = TP // 2
K, GDIM, EXAMPLES, PANEL = 8192, 32768, 1024, 512
HI = lax.Precision.HIGHEST
NT = (((1,), (1,)), ((), ()))
TN = (((0,), (0,)), ((), ()))
NN = (((1,), (0,)), ((), ()))


def wrap(value):
    value &= 0xFFFFFFFF
    return value - (1 << 32) if value >= (1 << 31) else value


C1, C2, C3 = -1640531535, 668265263, -2048144789
CUT1, CUT2, CUT3 = 5, 9, 13
C4 = wrap(-1028477387 << 8)


def slot_of(b):
    return 2 * (b % 2) + b // 2


def right_shift(value, amount):
    return lax.shift_right_logical(value, jnp.full_like(value, amount))


def split3(x):
    a = x.astype(jnp.bfloat16)
    r = x - a.astype(jnp.float32)
    b = r.astype(jnp.bfloat16)
    c = (r - b.astype(jnp.float32)).astype(jnp.bfloat16)
    return a, b, c

def dot3(x, y, dims):
    xa, xb, xc = split3(x)
    ya, yb, yc = split3(y)
    kx, ky = dims[0][0][0], dims[0][1][0]
    left = jnp.concatenate([xa, xa, xb, xa, xb, xc], axis=kx)
    right = jnp.concatenate([ya, yb, ya, yc, yb, ya], axis=ky)
    return lax.dot_general(left, right, dims, preferred_element_type=jnp.float32)

def base_inverse(s, hook):
    n = 128
    rowid = lax.broadcasted_iota(jnp.int32, (8, 128), 0)
    lane = lax.broadcasted_iota(jnp.int32, (8, 128), 1)
    top = [s[8 * i:8 * i + 8, :] for i in range(n // 8)]
    aug = [(lane == rowid + 8 * i).astype(jnp.float32) for i in range(n // 8)]
    done = []
    for m in range(n // 8):
        r, a = top[m], aug[m]
        v = [jnp.broadcast_to(r[:, 8 * m + k:8 * m + k + 1], (8, 128)) for k in range(8)]
        scale = jnp.zeros((8, 128), jnp.float32)
        for j in range(8):
            d = jnp.broadcast_to(v[j][j:j + 1, :], (8, 128))
            scale = jnp.where(rowid == j, lax.rsqrt(d), scale)
            if j < 7:
                f = jnp.where(rowid > j, v[j] / d, 0.0)
                for k in range(j + 1, 8):
                    v[k] = v[k] - f * jnp.broadcast_to(v[k][j:j + 1, :], (8, 128))
                r = r - f * jnp.broadcast_to(r[j:j + 1, :], (8, 128))
                a = a - f * jnp.broadcast_to(a[j:j + 1, :], (8, 128))
        r = r * scale
        a = a * scale
        done.append(a)
        hook(m)
        if m < n // 8 - 1:
            ra, rb, rc = split3(r)
            aa, ab, ac = split3(a)
            lo = 8 * (m + 1)
            left = jnp.concatenate([ra, ra, rb, ra, rb, rc], axis=0)
            right = jnp.concatenate([jnp.concatenate([x, y], axis=1) for x, y in
                                     ((ra, aa), (rb, ab), (ra, aa), (rc, ac), (rb, ab), (ra, aa))], axis=0)
            u = lax.dot_general(left, right, TN, preferred_element_type=jnp.float32)
            for i in range(m + 1, n // 8):
                top[i] = top[i] - u[8 * i:8 * i + 8, :128]
                aug[i] = aug[i] - u[8 * i:8 * i + 8, 128:]
    return jnp.concatenate(done, axis=0)

def factor_inverse(A, N, M, hook):
    for k in range(4):
        rk = slice(128 * k, 128 * k + 128)
        w = base_inverse(A[rk, rk], lambda m, k=k: hook(k, m))
        if k > 0:
            M[rk, :128 * k] = dot3(w, N[rk, :128 * k], (((1,), (0,)), ((), ())))
        M[rk, rk] = w
        if k < 3:
            M[rk, 128 * (k + 1):] = jnp.zeros((128, 512 - 128 * (k + 1)), jnp.float32)
            y = dot3(w, A[rk, 128 * (k + 1):], (((1,), (0,)), ((), ())))
            ym = M[rk, :128 * (k + 1)]
            for i in range(k + 1, 4):
                ri = slice(128 * i, 128 * i + 128)
                yi = y[:, 128 * (i - k - 1):128 * (i - k)]
                A[ri, 128 * i:] = A[ri, 128 * i:] - dot3(yi, y[:, 128 * (i - k - 1):], TN)
                up = dot3(yi, ym, TN)
                if k > 0:
                    N[ri, :128 * k] = N[ri, :128 * k] - up[:, :128 * k]
                N[ri, rk] = -up[:, 128 * k:]


def split2(x):
    a = x.astype(jnp.bfloat16)
    return a, (x - a.astype(jnp.float32)).astype(jnp.bfloat16)


def dot2(x, y, dims):
    xa, xb = split2(x)
    ya, yb = split2(y)

    def one(p, q):
        return lax.dot_general(p, q, dims, preferred_element_type=jnp.float32)

    return one(xa, ya) + (one(xa, yb) + one(xb, ya))


def whole_kernel(
    seed_ref, ridge_ref, grads_ref, sel_ref, pan, trail,
    chosen_ref, cvec_ref, sign_ref, parts, fp, fr, fc, prx, rx, A, N, M, X,
    ps, pr, ms, mr, pys, pyr, mys, myr, rps, rpr, pzs, pzr,
    rs_, rr_, ls_, lr_, ras, rar, rds, rdr, pas, par, pds, pdr, loc,
):
    z, t, b = lax.axis_index("ex"), lax.axis_index("tp"), lax.axis_index("blk")
    u, c = t // 2, t % 2
    slot = slot_of(b)
    scaling = jnp.float32(1.0 / math.sqrt(GDIM))
    pool, coords = grads_ref.shape
    pending = []

    def to(**axes):
        at = {"ex": z, "tp": t, "blk": b}
        at.update(axes)
        return (at["ex"], at["tp"], at["blk"])

    def copy(src, dst, send, recv, target):
        return pltpu.make_async_remote_copy(
            src_ref=src, dst_ref=dst, send_sem=send, recv_sem=recv,
            device_id=target, device_id_type=pl.DeviceIdType.MESH,
        )

    def go(src, dst, send, recv, target):
        one = copy(src, dst, send, recv, target)
        one.start()
        pending.append(one)
        return one

    def lanes(index):
        return pl.ds(pl.multiple_of(index * SB, SB), SB)

    tp_peers = [(d, lax.rem(t + d, TP)) for d in range(1, TP)]
    chip_peers = [(d, lax.rem(u + d, CHIPS) * 2 + c) for d in range(1, CHIPS)]
    blk_peers = [(d, lax.rem(b + d, BLK)) for d in range(1, BLK)]
    ex_peers = [(d, lax.rem(z + d, EX)) for d in range(1, EX)]
    other = u * 2 + 1 - c
    mate = to(ex=u, tp=2 * z + b // 2, blk=2 * c + b % 2)
    alone = jnp.logical_and(u == z, b // 2 == c)

    barrier = pltpu.get_barrier_semaphore()

    def greet(target):
        pl.semaphore_signal(barrier, inc=1, device_id=target, device_id_type=pl.DeviceIdType.MESH)

    for _, p in tp_peers:
        greet(to(tp=p))
    for _, p in blk_peers:
        greet(to(blk=p))
    for _, p in ex_peers:
        greet(to(ex=p))

    @pl.when(jnp.logical_not(alone))
    def _():
        greet(mate)

    hot = (lax.broadcasted_iota(jnp.int32, (pool, SB), 0) == sel_ref[...]).astype(jnp.float32)
    hot = hot.astype(jnp.bfloat16)
    for s in range(coords // 256):
        chosen_ref[pl.ds(s * 256, 256), :] = lax.dot_general(
            grads_ref[:, s * 256 : (s + 1) * 256], hot, TN, preferred_element_type=jnp.float32
        ).astype(jnp.bfloat16)
    cvec_ref[...] = (t * coords + lax.broadcasted_iota(jnp.int32, (8, coords), 1)) * jnp.int32(C1) + seed_ref[0]

    def product(block):
        first = block * PANEL + slot * SB

        def rows(r, carry):
            ids = first + r * 16 + lax.broadcasted_iota(jnp.int32, (8, 128), 0)
            low = ids * jnp.int32(C2)
            high = low + jnp.int32(wrap(8 * C2))
            start = pl.multiple_of(r * 16, 16)
            for s in range(coords // 128):
                at = cvec_ref[:, s * 128 : (s + 1) * 128]
                halves = []
                for f in (low, high):
                    h = at + f
                    h = (h ^ right_shift(h, 16)) * jnp.int32(C3)
                    h = (h ^ right_shift(h, 13)) * jnp.int32(C4)
                    h = h ^ (h << 16)
                    halves.append(jnp.where(h < 0, jnp.float32(-1), jnp.float32(1)))
                sign_ref[pl.ds(start, 16), s * 128 : (s + 1) * 128] = jnp.concatenate(halves, axis=0).astype(
                    jnp.bfloat16
                )
            return carry

        lax.fori_loop(0, SB // 16, rows, 0)
        out = jnp.dot(sign_ref[...], chosen_ref[...], preferred_element_type=jnp.float32)
        parts[block] = out.astype(jnp.bfloat16)

    product(0)
    greeted = len(tp_peers) + len(blk_peers) + len(ex_peers) + 1
    pl.semaphore_wait(barrier, greeted - alone.astype(jnp.int32))

    panel_in = []
    for d, p in tp_peers:
        rows16 = pl.ds(pl.multiple_of((p // 2) * 16, 16), 16)
        panel_in.append(go(parts.at[0, rows16, :], prx.at[d], ps.at[d], pr.at[d], to(tp=p)))

    def share(d):
        p = lax.rem(t + d, TP)
        return copy(parts.at[p], rx.at[d], ms.at[d], mr.at[d], to(tp=p))

    def blocks(lo, hi):
        def body(d, carry):
            p = lax.rem(t + d, TP)

            @pl.when(p != 0)
            def _():
                product(p)

            share(d).start()
            return carry

        lax.fori_loop(lo, hi, body, 0)

    blocks(1, CUT1)
    for one in panel_in:
        one.wait_recv()
    total = parts[0, pl.ds(pl.multiple_of(u * 16, 16), 16), :].astype(jnp.float32)
    for d in range(1, TP):
        total = total + prx[d].astype(jnp.float32)
    fp[slot, u, :, lanes(z)] = (total * scaling).astype(jnp.bfloat16)
    mine = fp.at[slot, u, :, lanes(z)]
    panel_y = [go(mine, mine, pys.at[d], pyr.at[d], to(blk=p)) for d, p in blk_peers]

    blocks(CUT1, CUT2)
    for one in panel_y:
        one.wait_recv()
    mine = fp.at[:, u, :, lanes(z)]
    panel_z = [go(mine, mine, pzs.at[d], pzr.at[d], to(ex=p)) for d, p in ex_peers]

    blocks(CUT2, CUT3)
    for one in panel_z:
        one.wait_recv()

    def panel_at(chip):
        return fp.at[pl.ds(2 * c, 2), chip]

    mine = panel_at(u)
    panel_a = [go(mine, mine, pas.at[d], par.at[d], to(tp=p)) for d, p in chip_peers]

    blocks(CUT3, TP)

    @pl.when(t != 0)
    def _():
        product(t)

    for d in range(1, TP):
        share(d).wait_recv()
    total = parts[t].astype(jnp.float32)
    for d in range(1, TP):
        total = total + rx[d].astype(jnp.float32)
    fc[lanes(slot), lanes(z)] = (total * scaling).astype(jnp.bfloat16)
    mine = fc.at[lanes(slot), lanes(z)]
    main_y = [None] + [go(mine, mine, mys.at[d], myr.at[d], to(blk=p)) for d, p in blk_peers]

    row_slot = fr.at[lanes(b // 2), lanes(z)]
    moved = copy(mine, row_slot, rps, rpr, mate)

    @pl.when(alone)
    def _():
        pltpu.make_async_copy(mine, row_slot, loc).start()

    @pl.when(jnp.logical_not(alone))
    def _():
        moved.start()

    right, left = to(ex=lax.rem(z + 1, EX)), to(ex=lax.rem(z + EX - 1, EX))
    rights, lefts = {}, {}

    def piece(step, j):
        row = slot_of(lax.rem(b + BLK - j, BLK))
        return fc.at[lanes(row), lanes(lax.rem(z + step + EX, EX))]

    def pass_right(s, j):
        at = piece(-s, j)
        rights[s, j] = go(at, at, rs_.at[s, j], rr_.at[s, j], right)

    def pass_left(s, j):
        at = piece(s, j)
        lefts[s, j] = go(at, at, ls_.at[s, j], lr_.at[s, j], left)

    pass_right(0, 0)
    pass_left(0, 0)

    panel_over = []
    for d in range(1, CHIPS):
        panel_a[d - 1].wait_recv()
        at = panel_at(lax.rem(u + CHIPS - d, CHIPS))
        panel_over.append(go(at, at, pds.at[d], pdr.at[d], to(tp=other)))
    for one in panel_over:
        one.wait_recv()

    def along_blk():
        for j in range(1, BLK):
            main_y[j].wait_recv()
            pass_right(0, j)
            pass_left(0, j)

    def row_at(chip):
        return fr.at[lanes(c), lanes(chip)]

    rows_in, rows_over = [], []

    def rows_out():
        @pl.when(alone)
        def _():
            pltpu.make_async_copy(piece(0, 0), row_slot, loc).wait()

        @pl.when(jnp.logical_not(alone))
        def _():
            moved.wait_send()
            moved.wait_recv()

        mine = row_at(u)
        rows_in.extend(go(mine, mine, ras.at[d], rar.at[d], to(tp=p)) for d, p in chip_peers)
        rows_over.append(go(mine, mine, rds.at[0], rdr.at[0], to(tp=other)))

    def ring(s, js):
        for j in js:
            rights[s - 1, j].wait_recv()
            if s < EX // 2 - 1 or j < BLK // 2:
                pass_right(s, j)
            lefts[s - 1, j].wait_recv()
            if s < EX // 2 - 1 or j >= BLK // 2:
                pass_left(s, j)

    def rows_across():
        for d in range(1, CHIPS):
            rows_in[d - 1].wait_recv()
            at = row_at(lax.rem(u + CHIPS - d, CHIPS))
            rows_over.append(go(at, at, rds.at[d], rdr.at[d], to(tp=other)))

    actions = {
        (0, 12): (along_blk, rows_out),
        (1, 2): (lambda: ring(1, (0,)),),
        (1, 7): (lambda: ring(1, (1,)),),
        (1, 11): (lambda: ring(1, (2,)),),
        (1, 15): (lambda: ring(1, (3,)), lambda: ring(2, (0,))),
        (2, 3): (lambda: ring(2, (1,)),),
        (2, 7): (lambda: ring(2, (2,)),),
        (2, 11): (lambda: ring(2, (3,)), lambda: ring(3, (0,))),
        (2, 15): (lambda: ring(3, (1,)),),
        (3, 3): (lambda: ring(3, (2,)),),
        (3, 7): (lambda: ring(3, (3,)), rows_across),
    }

    def hook(k, m):
        for act in actions.get((k, m), ()):
            act()

    g = z * BLK + b
    inv = jnp.float32(1.0 / EXAMPLES)
    rv = ridge_ref[0]

    def gram(left_part, right_part, r0, c0):
        out = lax.dot_general(left_part, right_part, NT, preferred_element_type=jnp.float32) * inv
        rows_, cols_ = (lax.broadcasted_iota(jnp.int32, out.shape, k) for k in range(2))
        return out + jnp.where(rows_ + r0 == cols_ + c0, rv, 0.0)

    panel = fp[...].reshape(PANEL, EXAMPLES)
    A[...] = gram(panel, panel, 0, 0)
    factor_inverse(A, N, M, hook)

    last = EX // 2 - 1
    for j in range(BLK // 2):
        rights[last, j].wait_recv()
        lefts[last, BLK // 2 + j].wait_recv()
    for one in rows_over:
        one.wait_recv()
    for one in pending:
        one.wait_send()
    for d in range(1, TP):
        share(d).wait_send()

    panel = fp[...].reshape(PANEL, EXAMPLES)
    X[...] = dot2(M[...], gram(panel, fc[...], 0, t * PANEL), NN)
    first_tile = gram(fr[...], panel, g * 2 * SB, 0)
    own = gram(fr[...], fc[...], g * 2 * SB, t * PANEL)
    out = dot2(first_tile, M[...], NT)
    pan[...] = out
    trail[...] = own - dot2(out, X[...], NN)


def whole(seed, ridge, grads, sel):
    bf, f32 = jnp.bfloat16, jnp.float32
    coords = grads.shape[1]
    dma = pltpu.SemaphoreType.DMA
    sems = []
    for n in (TP, TP, BLK, BLK):
        sems += [dma((n,)), dma((n,))]
    sems += [dma, dma, dma((EX,)), dma((EX,))]
    sems += [dma((EX // 2, BLK))] * 4
    sems += [dma((CHIPS,))] * 8
    sems += [dma]
    vmem = pl.BlockSpec(memory_space=pltpu.VMEM)
    smem = pl.BlockSpec(memory_space=pltpu.SMEM)
    tile = jax.ShapeDtypeStruct((2 * SB, PANEL), f32)
    square = pltpu.VMEM((PANEL, PANEL), f32)
    return pl.pallas_call(
        whole_kernel,
        out_shape=(tile, tile),
        in_specs=[smem, smem, vmem, vmem],
        out_specs=(vmem, vmem),
        scratch_shapes=[
            pltpu.VMEM((coords, SB), bf),
            pltpu.VMEM((8, coords), jnp.int32),
            pltpu.VMEM((SB, coords), bf),
            pltpu.VMEM((TP, SB, SB), bf),
            pltpu.VMEM((BLK, CHIPS, 16, EXAMPLES), bf),
            pltpu.VMEM((2 * SB, EXAMPLES), bf),
            pltpu.VMEM((PANEL, EXAMPLES), bf),
            pltpu.VMEM((TP, 16, SB), bf),
            pltpu.VMEM((TP, SB, SB), bf),
            square, square, square, square,
            *sems,
        ],
        compiler_params=pltpu.CompilerParams(collective_id=0, has_side_effects=True),
        name="whole",
    )(seed, ridge, grads, sel)


def shards(gradients, selection, seed_value, ridge_value):
    return whole(seed_value, ridge_value, gradients, selection.reshape(1, SB))


def solution(mesh):
    in_specs = (P("ex", "tp"), P("ex"), P(), P())
    out_specs = (P(("ex", "blk"), None), P(("ex", "blk"), "tp"))
    return jax.shard_map(shards, mesh=mesh, in_specs=in_specs, out_specs=out_specs, check_vma=False)
```

```python
import math

import jax
import jax.numpy as jnp
from jax import lax
from jax.experimental import pallas as pl
from jax.experimental.pallas import tpu as pltpu
from jax.sharding import PartitionSpec as P

SB = 128
EX, TP, BLK = 8, 16, 4
CHIPS = TP // 2
K, GDIM, EXAMPLES, PANEL = 8192, 32768, 1024, 512
HI = lax.Precision.HIGHEST
NT = (((1,), (1,)), ((), ()))
TN = (((0,), (0,)), ((), ()))
NN = (((1,), (0,)), ((), ()))


def wrap(value):
    value &= 0xFFFFFFFF
    return value - (1 << 32) if value >= (1 << 31) else value


C1, C2, C3 = -1640531535, 668265263, -2048144789
CUT1, CUT2 = 6, 12
C4 = wrap(-1028477387 << 8)


def slot_of(b):
    return 2 * (b % 2) + b // 2


def right_shift(value, amount):
    return lax.shift_right_logical(value, jnp.full_like(value, amount))


def split3(x):
    a = x.astype(jnp.bfloat16)
    r = x - a.astype(jnp.float32)
    b = r.astype(jnp.bfloat16)
    c = (r - b.astype(jnp.float32)).astype(jnp.bfloat16)
    return a, b, c

def dot3(x, y, dims):
    xa, xb, xc = split3(x)
    ya, yb, yc = split3(y)
    kx, ky = dims[0][0][0], dims[0][1][0]
    left = jnp.concatenate([xa, xa, xb, xa, xb, xc], axis=kx)
    right = jnp.concatenate([ya, yb, ya, yc, yb, ya], axis=ky)
    return lax.dot_general(left, right, dims, preferred_element_type=jnp.float32)

def base_inverse(s, hook):
    n = 128
    steps = n // 8
    rowid = lax.broadcasted_iota(jnp.int32, (8, 128), 0)
    lane = lax.broadcasted_iota(jnp.int32, (8, 128), 1)
    top = [s[8 * i : 8 * i + 8, :] for i in range(steps)]
    aug = [(lane == rowid + 8 * i).astype(jnp.float32) for i in range(steps)]

    def across(x, k):
        return jnp.broadcast_to(x[:, k : k + 1], (8, 128))

    def down(x, j):
        return jnp.broadcast_to(x[j : j + 1, :], (8, 128))

    done = []
    for m in range(steps):
        r, a = top[m], aug[m]
        ahead = m + 1 < steps
        v = [across(r, 8 * m + k) for k in range(8)]
        if ahead:
            nr, na = top[m + 1], aug[m + 1]
            w = [across(nr, 8 * m + k) for k in range(8)]
        for j in range(8):
            root = lax.rsqrt(down(v[j], j))
            f = jnp.where(rowid > j, v[j] * root, 0.0)
            yr, ya = down(r, j) * root, down(a, j) * root
            if ahead:
                g = w[j] * root
            for k in range(j + 1, 8):
                q = down(v[k], j) * root
                v[k] = v[k] - f * q
                if ahead:
                    w[k] = w[k] - g * q
            r = jnp.where(rowid == j, yr, r - f * yr)
            a = jnp.where(rowid == j, ya, a - f * ya)
            if ahead:
                nr = nr - g * yr
                na = na - g * ya
        done.append(a)
        if ahead:
            top[m + 1], aug[m + 1] = nr, na
        if m + 2 < steps:
            ra, rb, rc = split3(r)
            aa, ab, ac = split3(a)
            left = jnp.concatenate([ra, ra, rb, ra, rb, rc], axis=0)
            right = jnp.concatenate(
                [
                    jnp.concatenate([x, y], axis=1)
                    for x, y in ((ra, aa), (rb, ab), (ra, aa), (rc, ac), (rb, ab), (ra, aa))
                ],
                axis=0,
            )
            out = lax.dot_general(left, right, TN, preferred_element_type=jnp.float32)
            for i in range(m + 2, steps):
                top[i] = top[i] - out[8 * i : 8 * i + 8, :128]
                aug[i] = aug[i] - out[8 * i : 8 * i + 8, 128:]
        hook(m)
    return jnp.concatenate(done, axis=0)


def factor_inverse(A, N, M, hook):
    for k in range(4):
        rk = slice(128 * k, 128 * k + 128)
        w = base_inverse(A[rk, rk], lambda m, k=k: hook(k, m))
        if k > 0:
            M[rk, :128 * k] = dot3(w, N[rk, :128 * k], (((1,), (0,)), ((), ())))
        M[rk, rk] = w
        if k < 3:
            M[rk, 128 * (k + 1):] = jnp.zeros((128, 512 - 128 * (k + 1)), jnp.float32)
            y = dot3(w, A[rk, 128 * (k + 1):], (((1,), (0,)), ((), ())))
            ym = M[rk, :128 * (k + 1)]
            for i in range(k + 1, 4):
                ri = slice(128 * i, 128 * i + 128)
                yi = y[:, 128 * (i - k - 1):128 * (i - k)]
                A[ri, 128 * i:] = A[ri, 128 * i:] - dot3(yi, y[:, 128 * (i - k - 1):], TN)
                up = dot3(yi, ym, TN)
                if k > 0:
                    N[ri, :128 * k] = N[ri, :128 * k] - up[:, :128 * k]
                N[ri, rk] = -up[:, 128 * k:]


def split2(x):
    a = x.astype(jnp.bfloat16)
    return a, (x - a.astype(jnp.float32)).astype(jnp.bfloat16)


def dot2(x, y, dims):
    xa, xb = split2(x)
    ya, yb = split2(y)

    def one(p, q):
        return lax.dot_general(p, q, dims, preferred_element_type=jnp.float32)

    return one(xa, ya) + (one(xa, yb) + one(xb, ya))


def whole_kernel(
    seed_ref, ridge_ref, grads_ref, sel_ref, pan, trail,
    chosen_ref, cvec_ref, sign_ref, parts, fp, fr, fc, prx, rx, A, N, M, X,
    ps, pr, ms, mr, pys, pyr, mys, myr, rps, rpr, pzs, pzr,
    rs_, rr_, ls_, lr_, ras, rar, rds, rdr, pas, par, pds, pdr, loc,
):
    z, t, b = lax.axis_index("ex"), lax.axis_index("tp"), lax.axis_index("blk")
    u, c = t // 2, t % 2
    slot = slot_of(b)
    scaling = jnp.float32(1.0 / math.sqrt(GDIM))
    pool, coords = grads_ref.shape
    pending = []

    def to(**axes):
        at = {"ex": z, "tp": t, "blk": b}
        at.update(axes)
        return (at["ex"], at["tp"], at["blk"])

    def copy(src, dst, send, recv, target):
        return pltpu.make_async_remote_copy(
            src_ref=src, dst_ref=dst, send_sem=send, recv_sem=recv,
            device_id=target, device_id_type=pl.DeviceIdType.MESH,
        )

    def go(src, dst, send, recv, target):
        one = copy(src, dst, send, recv, target)
        one.start()
        pending.append(one)
        return one

    def lanes(index):
        return pl.ds(pl.multiple_of(index * SB, SB), SB)

    tp_peers = [(d, lax.rem(t + d, TP)) for d in range(1, TP)]
    chip_peers = [(d, lax.rem(u + d, CHIPS) * 2 + c) for d in range(1, CHIPS)]
    blk_peers = [(d, lax.rem(b + d, BLK)) for d in range(1, BLK)]
    ex_peers = [(d, lax.rem(z + d, EX)) for d in range(1, EX)]
    other = u * 2 + 1 - c
    mate = to(ex=u, tp=2 * z + b // 2, blk=2 * c + b % 2)
    alone = jnp.logical_and(u == z, b // 2 == c)

    barrier = pltpu.get_barrier_semaphore()

    def greet(target):
        pl.semaphore_signal(barrier, inc=1, device_id=target, device_id_type=pl.DeviceIdType.MESH)

    for _, p in tp_peers:
        greet(to(tp=p))
    for _, p in blk_peers:
        greet(to(blk=p))
    for _, p in ex_peers:
        greet(to(ex=p))

    @pl.when(jnp.logical_not(alone))
    def _():
        greet(mate)

    hot = (lax.broadcasted_iota(jnp.int32, (pool, SB), 0) == sel_ref[...]).astype(jnp.float32)
    hot = hot.astype(jnp.bfloat16)
    for s in range(coords // 256):
        chosen_ref[pl.ds(s * 256, 256), :] = lax.dot_general(
            grads_ref[:, s * 256 : (s + 1) * 256], hot, TN, preferred_element_type=jnp.float32
        ).astype(jnp.bfloat16)
    cvec_ref[...] = (t * coords + lax.broadcasted_iota(jnp.int32, (8, coords), 1)) * jnp.int32(C1) + seed_ref[0]

    def product(block):
        first = block * PANEL + slot * SB

        def rows(r, carry):
            ids = first + r * 16 + lax.broadcasted_iota(jnp.int32, (8, 128), 0)
            low = ids * jnp.int32(C2)
            high = low + jnp.int32(wrap(8 * C2))
            start = pl.multiple_of(r * 16, 16)
            for s in range(coords // 128):
                at = cvec_ref[:, s * 128 : (s + 1) * 128]
                halves = []
                for f in (low, high):
                    h = at + f
                    h = (h ^ right_shift(h, 16)) * jnp.int32(C3)
                    h = (h ^ right_shift(h, 13)) * jnp.int32(C4)
                    h = h ^ (h << 16)
                    halves.append(jnp.where(h < 0, jnp.float32(-1), jnp.float32(1)))
                sign_ref[pl.ds(start, 16), s * 128 : (s + 1) * 128] = jnp.concatenate(halves, axis=0).astype(
                    jnp.bfloat16
                )
            return carry

        lax.fori_loop(0, SB // 16, rows, 0)
        out = jnp.dot(sign_ref[...], chosen_ref[...], preferred_element_type=jnp.float32)
        parts[block] = out.astype(jnp.bfloat16)

    product(0)
    greeted = len(tp_peers) + len(blk_peers) + len(ex_peers) + 1
    pl.semaphore_wait(barrier, greeted - alone.astype(jnp.int32))

    panel_in = []
    for d, p in tp_peers:
        rows16 = pl.ds(pl.multiple_of((p // 2) * 16, 16), 16)
        panel_in.append(go(parts.at[0, rows16, :], prx.at[d], ps.at[d], pr.at[d], to(tp=p)))

    def share(d):
        p = lax.rem(t + d, TP)
        return copy(parts.at[p], rx.at[d], ms.at[d], mr.at[d], to(tp=p))

    def blocks(lo, hi):
        def body(d, carry):
            p = lax.rem(t + d, TP)

            @pl.when(p != 0)
            def _():
                product(p)

            share(d).start()
            return carry

        lax.fori_loop(lo, hi, body, 0)

    blocks(1, CUT1)
    for one in panel_in:
        one.wait_recv()
    total = parts[0, pl.ds(pl.multiple_of(u * 16, 16), 16), :].astype(jnp.float32)
    for d in range(1, TP):
        total = total + prx[d].astype(jnp.float32)
    fp[slot, u, :, lanes(z)] = (total * scaling).astype(jnp.bfloat16)
    mine = fp.at[slot, u, :, lanes(z)]
    panel_y = [go(mine, mine, pys.at[d], pyr.at[d], to(blk=p)) for d, p in blk_peers]

    blocks(CUT1, CUT2)
    for one in panel_y:
        one.wait_recv()
    mine = fp.at[:, u, :, lanes(z)]
    panel_z = [go(mine, mine, pzs.at[d], pzr.at[d], to(ex=p)) for d, p in ex_peers]

    blocks(CUT2, TP)

    @pl.when(t != 0)
    def _():
        product(t)

    for d in range(1, TP):
        share(d).wait_recv()
    total = parts[t].astype(jnp.float32)
    for d in range(1, TP):
        total = total + rx[d].astype(jnp.float32)
    fc[lanes(slot), lanes(z)] = (total * scaling).astype(jnp.bfloat16)
    mine = fc.at[lanes(slot), lanes(z)]
    main_y = [None] + [go(mine, mine, mys.at[d], myr.at[d], to(blk=p)) for d, p in blk_peers]

    row_slot = fr.at[lanes(b // 2), lanes(z)]
    moved = copy(mine, row_slot, rps, rpr, mate)

    @pl.when(alone)
    def _():
        pltpu.make_async_copy(mine, row_slot, loc).start()

    @pl.when(jnp.logical_not(alone))
    def _():
        moved.start()

    right, left = to(ex=lax.rem(z + 1, EX)), to(ex=lax.rem(z + EX - 1, EX))
    rights, lefts = {}, {}

    def piece(step, j):
        row = slot_of(lax.rem(b + BLK - j, BLK))
        return fc.at[lanes(row), lanes(lax.rem(z + step + EX, EX))]

    def pass_right(s, j):
        at = piece(-s, j)
        rights[s, j] = go(at, at, rs_.at[s, j], rr_.at[s, j], right)

    def pass_left(s, j):
        at = piece(s, j)
        lefts[s, j] = go(at, at, ls_.at[s, j], lr_.at[s, j], left)

    pass_right(0, 0)
    pass_left(0, 0)

    for one in panel_z:
        one.wait_recv()

    def panel_at(chip):
        return fp.at[pl.ds(2 * c, 2), chip]

    mine = panel_at(u)
    panel_a = [go(mine, mine, pas.at[d], par.at[d], to(tp=p)) for d, p in chip_peers]

    def along_blk():
        for j in range(1, BLK):
            main_y[j].wait_recv()
            pass_right(0, j)
            pass_left(0, j)

    def row_at(chip):
        return fr.at[lanes(c), lanes(chip)]

    rows_in, rows_over = [], []

    def rows_out():
        @pl.when(alone)
        def _():
            pltpu.make_async_copy(piece(0, 0), row_slot, loc).wait()

        @pl.when(jnp.logical_not(alone))
        def _():
            moved.wait_send()
            moved.wait_recv()

        mine = row_at(u)
        rows_in.extend(go(mine, mine, ras.at[d], rar.at[d], to(tp=p)) for d, p in chip_peers)
        rows_over.append(go(mine, mine, rds.at[0], rdr.at[0], to(tp=other)))

    def ring(s, js):
        for j in js:
            rights[s - 1, j].wait_recv()
            if s < EX // 2 - 1 or j < BLK // 2:
                pass_right(s, j)
            lefts[s - 1, j].wait_recv()
            if s < EX // 2 - 1 or j >= BLK // 2:
                pass_left(s, j)

    def rows_across():
        for d in range(1, CHIPS):
            rows_in[d - 1].wait_recv()
            at = row_at(lax.rem(u + CHIPS - d, CHIPS))
            rows_over.append(go(at, at, rds.at[d], rdr.at[d], to(tp=other)))

    along_blk()
    ring(1, (0,))

    panel_over = []
    for d in range(1, CHIPS):
        panel_a[d - 1].wait_recv()
        at = panel_at(lax.rem(u + CHIPS - d, CHIPS))
        panel_over.append(go(at, at, pds.at[d], pdr.at[d], to(tp=other)))
    for one in panel_over:
        one.wait_recv()

    actions = {
        (0, 3): (rows_out, lambda: ring(1, (1,))),
        (0, 7): (lambda: ring(1, (2,)),),
        (0, 11): (lambda: ring(1, (3,)),),
        (1, 0): (lambda: ring(2, (0,)),),
        (1, 3): (lambda: ring(2, (1,)),),
        (1, 6): (lambda: ring(2, (2,)),),
        (1, 9): (lambda: ring(2, (3,)),),
        (1, 14): (lambda: ring(3, (0,)),),
        (2, 2): (lambda: ring(3, (1,)),),
        (2, 5): (lambda: ring(3, (2,)),),
        (2, 8): (lambda: ring(3, (3,)),),
        (2, 10): (rows_across,),
    }

    def hook(k, m):
        for act in actions.get((k, m), ()):
            act()

    g = z * BLK + b
    inv = jnp.float32(1.0 / EXAMPLES)
    rv = ridge_ref[0]

    def gram(left_part, right_part, r0, c0):
        out = lax.dot_general(left_part, right_part, NT, preferred_element_type=jnp.float32) * inv
        rows_, cols_ = (lax.broadcasted_iota(jnp.int32, out.shape, k) for k in range(2))
        return out + jnp.where(rows_ + r0 == cols_ + c0, rv, 0.0)

    panel = fp[...].reshape(PANEL, EXAMPLES)
    A[...] = gram(panel, panel, 0, 0)
    factor_inverse(A, N, M, hook)

    last = EX // 2 - 1
    for j in range(BLK // 2):
        rights[last, j].wait_recv()
        lefts[last, BLK // 2 + j].wait_recv()
    for one in rows_over:
        one.wait_recv()
    for one in pending:
        one.wait_send()
    for d in range(1, TP):
        share(d).wait_send()

    panel = fp[...].reshape(PANEL, EXAMPLES)
    X[...] = dot2(M[...], gram(panel, fc[...], 0, t * PANEL), NN)
    first_tile = gram(fr[...], panel, g * 2 * SB, 0)
    own = gram(fr[...], fc[...], g * 2 * SB, t * PANEL)
    out = dot2(first_tile, M[...], NT)
    pan[...] = out
    trail[...] = own - dot2(out, X[...], NN)


def whole(seed, ridge, grads, sel):
    bf, f32 = jnp.bfloat16, jnp.float32
    coords = grads.shape[1]
    dma = pltpu.SemaphoreType.DMA
    sems = []
    for n in (TP, TP, BLK, BLK):
        sems += [dma((n,)), dma((n,))]
    sems += [dma, dma, dma((EX,)), dma((EX,))]
    sems += [dma((EX // 2, BLK))] * 4
    sems += [dma((CHIPS,))] * 8
    sems += [dma]
    vmem = pl.BlockSpec(memory_space=pltpu.VMEM)
    smem = pl.BlockSpec(memory_space=pltpu.SMEM)
    tile = jax.ShapeDtypeStruct((2 * SB, PANEL), f32)
    square = pltpu.VMEM((PANEL, PANEL), f32)
    return pl.pallas_call(
        whole_kernel,
        out_shape=(tile, tile),
        in_specs=[smem, smem, vmem, vmem],
        out_specs=(vmem, vmem),
        scratch_shapes=[
            pltpu.VMEM((coords, SB), bf),
            pltpu.VMEM((8, coords), jnp.int32),
            pltpu.VMEM((SB, coords), bf),
            pltpu.VMEM((TP, SB, SB), bf),
            pltpu.VMEM((BLK, CHIPS, 16, EXAMPLES), bf),
            pltpu.VMEM((2 * SB, EXAMPLES), bf),
            pltpu.VMEM((PANEL, EXAMPLES), bf),
            pltpu.VMEM((TP, 16, SB), bf),
            pltpu.VMEM((TP, SB, SB), bf),
            square, square, square, square,
            *sems,
        ],
        compiler_params=pltpu.CompilerParams(collective_id=0, has_side_effects=True),
        name="whole",
    )(seed, ridge, grads, sel)


def shards(gradients, selection, seed_value, ridge_value):
    return whole(seed_value, ridge_value, gradients, selection.reshape(1, SB))


def solution(mesh):
    in_specs = (P("ex", "tp"), P("ex"), P(), P())
    out_specs = (P(("ex", "blk"), None), P(("ex", "blk"), "tp"))
    return jax.shard_map(shards, mesh=mesh, in_specs=in_specs, out_specs=out_specs, check_vma=False)
```

```python
import math

import jax
import jax.numpy as jnp
from jax import lax
from jax.experimental import pallas as pl
from jax.experimental.pallas import tpu as pltpu
from jax.sharding import PartitionSpec as P

SB = 128
EX, TP, BLK = 8, 16, 4
CHIPS = TP // 2
K, GDIM, EXAMPLES, PANEL = 8192, 32768, 1024, 512
HI = lax.Precision.HIGHEST
NT = (((1,), (1,)), ((), ()))
TN = (((0,), (0,)), ((), ()))
NN = (((1,), (0,)), ((), ()))


def wrap(value):
    value &= 0xFFFFFFFF
    return value - (1 << 32) if value >= (1 << 31) else value


C1, C2, C3 = -1640531535, 668265263, -2048144789
CUT1, CUT2 = 6, 11
C4 = wrap(-1028477387 << 8)


def slot_of(b):
    return 2 * (b % 2) + b // 2


def right_shift(value, amount):
    return lax.shift_right_logical(value, jnp.full_like(value, amount))


def split3(x):
    a = x.astype(jnp.bfloat16)
    r = x - a.astype(jnp.float32)
    b = r.astype(jnp.bfloat16)
    c = (r - b.astype(jnp.float32)).astype(jnp.bfloat16)
    return a, b, c

def dot3(x, y, dims):
    xa, xb, xc = split3(x)
    ya, yb, yc = split3(y)
    kx, ky = dims[0][0][0], dims[0][1][0]
    left = jnp.concatenate([xa, xa, xb, xa, xb, xc], axis=kx)
    right = jnp.concatenate([ya, yb, ya, yc, yb, ya], axis=ky)
    return lax.dot_general(left, right, dims, preferred_element_type=jnp.float32)

def base_inverse(s, hook):
    n = 128
    steps = n // 8
    rowid = lax.broadcasted_iota(jnp.int32, (8, 128), 0)
    lane = lax.broadcasted_iota(jnp.int32, (8, 128), 1)
    top = [s[8 * i : 8 * i + 8, :] for i in range(steps)]
    aug = [(lane == rowid + 8 * i).astype(jnp.float32) for i in range(steps)]

    def across(x, k):
        return jnp.broadcast_to(x[:, k : k + 1], (8, 128))

    def down(x, j):
        return jnp.broadcast_to(x[j : j + 1, :], (8, 128))

    done = []
    for m in range(steps):
        r, a = top[m], aug[m]
        ahead = m + 1 < steps
        v = [across(r, 8 * m + k) for k in range(8)]
        if ahead:
            nr, na = top[m + 1], aug[m + 1]
            w = [across(nr, 8 * m + k) for k in range(8)]
        for j in range(8):
            root = lax.rsqrt(down(v[j], j))
            f = jnp.where(rowid > j, v[j] * root, 0.0)
            yr, ya = down(r, j) * root, down(a, j) * root
            if ahead:
                g = w[j] * root
            for k in range(j + 1, 8):
                q = down(v[k], j) * root
                v[k] = v[k] - f * q
                if ahead:
                    w[k] = w[k] - g * q
            r = jnp.where(rowid == j, yr, r - f * yr)
            a = jnp.where(rowid == j, ya, a - f * ya)
            if ahead:
                nr = nr - g * yr
                na = na - g * ya
        done.append(a)
        if ahead:
            top[m + 1], aug[m + 1] = nr, na
        if m + 2 < steps:
            ra, rb, rc = split3(r)
            aa, ab, ac = split3(a)
            left = jnp.concatenate([ra, ra, rb, ra, rb, rc], axis=0)
            right = jnp.concatenate(
                [
                    jnp.concatenate([x, y], axis=1)
                    for x, y in ((ra, aa), (rb, ab), (ra, aa), (rc, ac), (rb, ab), (ra, aa))
                ],
                axis=0,
            )
            out = lax.dot_general(left, right, TN, preferred_element_type=jnp.float32)
            for i in range(m + 2, steps):
                top[i] = top[i] - out[8 * i : 8 * i + 8, :128]
                aug[i] = aug[i] - out[8 * i : 8 * i + 8, 128:]
        hook(m)
    return jnp.concatenate(done, axis=0)


def factor_inverse(A, N, M, hook):
    for k in range(4):
        rk = slice(128 * k, 128 * k + 128)
        w = base_inverse(A[rk, rk], lambda m, k=k: hook(k, m))
        if k > 0:
            M[rk, :128 * k] = dot3(w, N[rk, :128 * k], (((1,), (0,)), ((), ())))
        M[rk, rk] = w
        if k < 3:
            M[rk, 128 * (k + 1):] = jnp.zeros((128, 512 - 128 * (k + 1)), jnp.float32)
            y = dot3(w, A[rk, 128 * (k + 1):], (((1,), (0,)), ((), ())))
            ym = M[rk, :128 * (k + 1)]
            for i in range(k + 1, 4):
                ri = slice(128 * i, 128 * i + 128)
                yi = y[:, 128 * (i - k - 1):128 * (i - k)]
                A[ri, 128 * i:] = A[ri, 128 * i:] - dot3(yi, y[:, 128 * (i - k - 1):], TN)
                up = dot3(yi, ym, TN)
                if k > 0:
                    N[ri, :128 * k] = N[ri, :128 * k] - up[:, :128 * k]
                N[ri, rk] = -up[:, 128 * k:]


def split2(x):
    a = x.astype(jnp.bfloat16)
    return a, (x - a.astype(jnp.float32)).astype(jnp.bfloat16)


def dot2(x, y, dims):
    xa, xb = split2(x)
    ya, yb = split2(y)

    def one(p, q):
        return lax.dot_general(p, q, dims, preferred_element_type=jnp.float32)

    return one(xa, ya) + (one(xa, yb) + one(xb, ya))


def whole_kernel(
    seed_ref, ridge_ref, grads_hbm, sel_ref, pan, trail,
    grads_ref, T, chosen_ref, cvec_ref, sign_ref, parts, fp, fr, fc, prx, rx, A, N, M, X,
    ps, pr, ms, mr, pys, pyr, mys, myr, rps, rpr, pzs, pzr,
    rs_, rr_, ls_, lr_, ras, rar, rds, rdr, pas, par, pds, pdr, loc, fetched,
):
    z, t, b = lax.axis_index("ex"), lax.axis_index("tp"), lax.axis_index("blk")
    u, c = t // 2, t % 2
    slot = slot_of(b)
    scaling = jnp.float32(1.0 / math.sqrt(GDIM))
    pool, coords = grads_ref.shape
    pending = []

    def to(**axes):
        at = {"ex": z, "tp": t, "blk": b}
        at.update(axes)
        return (at["ex"], at["tp"], at["blk"])

    def copy(src, dst, send, recv, target):
        return pltpu.make_async_remote_copy(
            src_ref=src, dst_ref=dst, send_sem=send, recv_sem=recv,
            device_id=target, device_id_type=pl.DeviceIdType.MESH,
        )

    def go(src, dst, send, recv, target):
        one = copy(src, dst, send, recv, target)
        one.start()
        pending.append(one)
        return one

    def lanes(index):
        return pl.ds(pl.multiple_of(index * SB, SB), SB)

    tp_peers = [(d, lax.rem(t + d, TP)) for d in range(1, TP)]
    chip_peers = [(d, lax.rem(u + d, CHIPS) * 2 + c) for d in range(1, CHIPS)]
    blk_peers = [(d, lax.rem(b + d, BLK)) for d in range(1, BLK)]
    ex_peers = [(d, lax.rem(z + d, EX)) for d in range(1, EX)]
    other = u * 2 + 1 - c
    mate = to(ex=u, tp=2 * z + b // 2, blk=2 * c + b % 2)
    alone = jnp.logical_and(u == z, b // 2 == c)

    barrier = pltpu.get_barrier_semaphore()

    def greet(target):
        pl.semaphore_signal(barrier, inc=1, device_id=target, device_id_type=pl.DeviceIdType.MESH)

    for _, p in tp_peers:
        greet(to(tp=p))
    for _, p in blk_peers:
        greet(to(blk=p))
    for _, p in ex_peers:
        greet(to(ex=p))

    fetch = pltpu.make_async_copy(grads_hbm, grads_ref, fetched)
    fetch.start()
    hot = (lax.broadcasted_iota(jnp.int32, (pool, SB), 0) == sel_ref[...]).astype(jnp.float32)
    hot = hot.astype(jnp.bfloat16)
    cvec_ref[...] = (t * coords + lax.broadcasted_iota(jnp.int32, (8, coords), 1)) * jnp.int32(C1) + seed_ref[0]
    fetch.wait()
    for s in range(coords // 256):
        chosen_ref[pl.ds(s * 256, 256), :] = lax.dot_general(
            grads_ref[:, s * 256 : (s + 1) * 256], hot, TN, preferred_element_type=jnp.float32
        ).astype(jnp.bfloat16)

    def product(block):
        first = block * PANEL + slot * SB

        def rows(r, carry):
            ids = first + r * 16 + lax.broadcasted_iota(jnp.int32, (8, 128), 0)
            low = ids * jnp.int32(C2)
            high = low + jnp.int32(wrap(8 * C2))
            start = pl.multiple_of(r * 16, 16)
            for s in range(coords // 128):
                at = cvec_ref[:, s * 128 : (s + 1) * 128]
                halves = []
                for f in (low, high):
                    h = at + f
                    h = (h ^ right_shift(h, 16)) * jnp.int32(C3)
                    h = (h ^ right_shift(h, 13)) * jnp.int32(C4)
                    h = h ^ (h << 16)
                    halves.append(jnp.where(h < 0, jnp.float32(-1), jnp.float32(1)))
                sign_ref[pl.ds(start, 16), s * 128 : (s + 1) * 128] = jnp.concatenate(halves, axis=0).astype(
                    jnp.bfloat16
                )
            return carry

        lax.fori_loop(0, SB // 16, rows, 0)
        out = jnp.dot(sign_ref[...], chosen_ref[...], preferred_element_type=jnp.float32)
        parts[block] = out.astype(jnp.bfloat16)

    product(0)
    pl.semaphore_wait(barrier, len(tp_peers) + len(blk_peers) + len(ex_peers))

    panel_in = []
    for d, p in tp_peers:
        rows16 = pl.ds(pl.multiple_of((p // 2) * 16, 16), 16)
        panel_in.append(go(parts.at[0, rows16, :], prx.at[d], ps.at[d], pr.at[d], to(tp=p)))

    def share(d):
        p = lax.rem(t + d, TP)
        return copy(parts.at[p], rx.at[d], ms.at[d], mr.at[d], to(tp=p))

    def blocks(lo, hi):
        def body(d, carry):
            p = lax.rem(t + d, TP)

            @pl.when(p != 0)
            def _():
                product(p)

            share(d).start()
            return carry

        lax.fori_loop(lo, hi, body, 0)

    blocks(1, CUT1)
    for one in panel_in:
        one.wait_recv()
    total = parts[0, pl.ds(pl.multiple_of(u * 16, 16), 16), :].astype(jnp.float32)
    for d in range(1, TP):
        total = total + prx[d].astype(jnp.float32)
    fp[slot, u, :, lanes(z)] = (total * scaling).astype(jnp.bfloat16)
    mine = fp.at[slot, u, :, lanes(z)]
    panel_y = [go(mine, mine, pys.at[d], pyr.at[d], to(blk=p)) for d, p in blk_peers]

    blocks(CUT1, CUT2)
    for one in panel_y:
        one.wait_recv()
    mine = fp.at[:, u, :, lanes(z)]
    panel_z = [go(mine, mine, pzs.at[d], pzr.at[d], to(ex=p)) for d, p in ex_peers]

    blocks(CUT2, TP)

    @pl.when(t != 0)
    def _():
        product(t)

    for one in panel_z:
        one.wait_recv()

    def panel_at(chip):
        return fp.at[pl.ds(2 * c, 2), chip]

    mine = panel_at(u)
    panel_a = [go(mine, mine, pas.at[d], par.at[d], to(tp=p)) for d, p in chip_peers]

    for d in range(1, TP):
        share(d).wait_recv()
    total = parts[t].astype(jnp.float32)
    for d in range(1, TP):
        total = total + rx[d].astype(jnp.float32)
    fc[lanes(slot), lanes(z)] = (total * scaling).astype(jnp.bfloat16)
    mine = fc.at[lanes(slot), lanes(z)]
    main_y = [None] + [go(mine, mine, mys.at[d], myr.at[d], to(blk=p)) for d, p in blk_peers]

    row_slot = fr.at[lanes(b // 2), lanes(z)]
    moved = copy(mine, row_slot, rps, rpr, mate)

    right, left = to(ex=lax.rem(z + 1, EX)), to(ex=lax.rem(z + EX - 1, EX))
    rights, lefts = {}, {}

    def piece(step, j):
        row = slot_of(lax.rem(b + BLK - j, BLK))
        return fc.at[lanes(row), lanes(lax.rem(z + step + EX, EX))]

    def pass_right(s, j):
        at = piece(-s, j)
        rights[s, j] = go(at, at, rs_.at[s, j], rr_.at[s, j], right)

    def pass_left(s, j):
        at = piece(s, j)
        lefts[s, j] = go(at, at, ls_.at[s, j], lr_.at[s, j], left)

    pass_right(0, 0)
    pass_left(0, 0)

    def along_blk():
        for j in range(1, BLK):
            main_y[j].wait_recv()
            pass_right(0, j)
            pass_left(0, j)

    def row_at(chip):
        return fr.at[lanes(c), lanes(chip)]

    rows_in, rows_over = [], []

    def rows_out():
        @pl.when(alone)
        def _():
            pltpu.make_async_copy(piece(0, 0), row_slot, loc).wait()

        @pl.when(jnp.logical_not(alone))
        def _():
            moved.wait_send()
            moved.wait_recv()

        mine = row_at(u)
        rows_in.extend(go(mine, mine, ras.at[d], rar.at[d], to(tp=p)) for d, p in chip_peers)
        rows_over.append(go(mine, mine, rds.at[0], rdr.at[0], to(tp=other)))

    def ring(s, js):
        for j in js:
            rights[s - 1, j].wait_recv()
            if s < EX // 2 - 1 or j < BLK // 2:
                pass_right(s, j)
            lefts[s - 1, j].wait_recv()
            if s < EX // 2 - 1 or j >= BLK // 2:
                pass_left(s, j)

    def rows_across():
        for d in range(1, CHIPS):
            rows_in[d - 1].wait_recv()
            at = row_at(lax.rem(u + CHIPS - d, CHIPS))
            rows_over.append(go(at, at, rds.at[d], rdr.at[d], to(tp=other)))

    along_blk()
    ring(1, (0,))

    panel_over = []
    for d in range(1, CHIPS):
        panel_a[d - 1].wait_recv()
        at = panel_at(lax.rem(u + CHIPS - d, CHIPS))
        panel_over.append(go(at, at, pds.at[d], pdr.at[d], to(tp=other)))
    for one in panel_over:
        one.wait_recv()

    @pl.when(alone)
    def _():
        pltpu.make_async_copy(piece(0, 0), row_slot, loc).start()

    @pl.when(jnp.logical_not(alone))
    def _():
        moved.start()

    def columns_here():
        last = EX // 2 - 1
        for j in range(BLK // 2):
            rights[last, j].wait_recv()
            lefts[last, BLK // 2 + j].wait_recv()
        T[...] = gram(fp[...].reshape(PANEL, EXAMPLES), fc[...], 0, t * PANEL)

    actions = {
        (0, 3): (lambda: ring(1, (1,)),),
        (0, 7): (lambda: ring(1, (2,)),),
        (0, 11): (lambda: ring(1, (3,)),),
        (1, 0): (lambda: ring(2, (0,)),),
        (1, 3): (lambda: ring(2, (1,)),),
        (1, 6): (lambda: ring(2, (2,)),),
        (1, 8): (rows_out,),
        (1, 9): (lambda: ring(2, (3,)),),
        (1, 14): (lambda: ring(3, (0,)),),
        (2, 2): (lambda: ring(3, (1,)),),
        (2, 5): (lambda: ring(3, (2,)),),
        (2, 8): (lambda: ring(3, (3,)),),
        (3, 1): (columns_here,),
        (3, 6): (rows_across,),
    }

    def hook(k, m):
        for act in actions.get((k, m), ()):
            act()

    g = z * BLK + b
    inv = jnp.float32(1.0 / EXAMPLES)
    rv = ridge_ref[0]

    def gram(left_part, right_part, r0, c0):
        out = lax.dot_general(left_part, right_part, NT, preferred_element_type=jnp.float32) * inv
        rows_, cols_ = (lax.broadcasted_iota(jnp.int32, out.shape, k) for k in range(2))
        return out + jnp.where(rows_ + r0 == cols_ + c0, rv, 0.0)

    panel = fp[...].reshape(PANEL, EXAMPLES)
    A[...] = gram(panel, panel, 0, 0)
    factor_inverse(A, N, M, hook)

    for one in rows_over:
        one.wait_recv()
    for one in pending:
        one.wait_send()
    for d in range(1, TP):
        share(d).wait_send()

    panel = fp[...].reshape(PANEL, EXAMPLES)
    X[...] = dot2(M[...], T[...], NN)
    first_tile = gram(fr[...], panel, g * 2 * SB, 0)
    own = gram(fr[...], fc[...], g * 2 * SB, t * PANEL)
    out = dot2(first_tile, M[...], NT)
    pan[...] = out
    trail[...] = own - dot2(out, X[...], NN)


def whole(seed, ridge, grads, sel):
    bf, f32 = jnp.bfloat16, jnp.float32
    coords = grads.shape[1]
    dma = pltpu.SemaphoreType.DMA
    sems = []
    for n in (TP, TP, BLK, BLK):
        sems += [dma((n,)), dma((n,))]
    sems += [dma, dma, dma((EX,)), dma((EX,))]
    sems += [dma((EX // 2, BLK))] * 4
    sems += [dma((CHIPS,))] * 8
    sems += [dma, dma]
    vmem = pl.BlockSpec(memory_space=pltpu.VMEM)
    smem = pl.BlockSpec(memory_space=pltpu.SMEM)
    tile = jax.ShapeDtypeStruct((2 * SB, PANEL), f32)
    square = pltpu.VMEM((PANEL, PANEL), f32)
    return pl.pallas_call(
        whole_kernel,
        out_shape=(tile, tile),
        in_specs=[smem, smem, pl.BlockSpec(memory_space=pl.ANY), vmem],
        out_specs=(vmem, vmem),
        scratch_shapes=[
            pltpu.VMEM(grads.shape, bf),
            square,
            pltpu.VMEM((coords, SB), bf),
            pltpu.VMEM((8, coords), jnp.int32),
            pltpu.VMEM((SB, coords), bf),
            pltpu.VMEM((TP, SB, SB), bf),
            pltpu.VMEM((BLK, CHIPS, 16, EXAMPLES), bf),
            pltpu.VMEM((2 * SB, EXAMPLES), bf),
            pltpu.VMEM((PANEL, EXAMPLES), bf),
            pltpu.VMEM((TP, 16, SB), bf),
            pltpu.VMEM((TP, SB, SB), bf),
            square, square, square, square,
            *sems,
        ],
        compiler_params=pltpu.CompilerParams(collective_id=0, has_side_effects=True),
        name="whole",
    )(seed, ridge, grads, sel)


def shards(gradients, selection, seed_value, ridge_value):
    return whole(seed_value, ridge_value, gradients, selection.reshape(1, SB))


def solution(mesh):
    in_specs = (P("ex", "tp"), P("ex"), P(), P())
    out_specs = (P(("ex", "blk"), None), P(("ex", "blk"), "tp"))
    return jax.shard_map(shards, mesh=mesh, in_specs=in_specs, out_specs=out_specs, check_vma=False)
```

```python
import math

import jax
import jax.numpy as jnp
from jax import lax
from jax.experimental import pallas as pl
from jax.experimental.pallas import tpu as pltpu
from jax.sharding import PartitionSpec as P

SB = 128
EX, TP, BLK = 8, 16, 4
CHIPS = TP // 2
K, GDIM, EXAMPLES, PANEL = 8192, 32768, 1024, 512
HI = lax.Precision.HIGHEST
NT = (((1,), (1,)), ((), ()))
TN = (((0,), (0,)), ((), ()))
NN = (((1,), (0,)), ((), ()))


def wrap(value):
    value &= 0xFFFFFFFF
    return value - (1 << 32) if value >= (1 << 31) else value


C1, C2, C3 = -1640531535, 668265263, -2048144789
CUT1, CUT2 = 6, 11
C4 = wrap(-1028477387 << 8)


def slot_of(b):
    return 2 * (b % 2) + b // 2


def right_shift(value, amount):
    return lax.shift_right_logical(value, jnp.full_like(value, amount))


def split3(x):
    a = x.astype(jnp.bfloat16)
    r = x - a.astype(jnp.float32)
    b = r.astype(jnp.bfloat16)
    c = (r - b.astype(jnp.float32)).astype(jnp.bfloat16)
    return a, b, c

def dot3(x, y, dims):
    xa, xb, xc = split3(x)
    ya, yb, yc = split3(y)
    kx, ky = dims[0][0][0], dims[0][1][0]
    left = jnp.concatenate([xa, xa, xb, xa, xb, xc], axis=kx)
    right = jnp.concatenate([ya, yb, ya, yc, yb, ya], axis=ky)
    return lax.dot_general(left, right, dims, preferred_element_type=jnp.float32)

def base_inverse(s, hook):
    n = 128
    steps = n // 8
    rowid = lax.broadcasted_iota(jnp.int32, (8, 128), 0)
    lane = lax.broadcasted_iota(jnp.int32, (8, 128), 1)
    top = [s[8 * i : 8 * i + 8, :] for i in range(steps)]
    aug = [(lane == rowid + 8 * i).astype(jnp.float32) for i in range(steps)]

    def across(x, k):
        return jnp.broadcast_to(x[:, k : k + 1], (8, 128))

    def down(x, j):
        return jnp.broadcast_to(x[j : j + 1, :], (8, 128))

    done = []
    for m in range(steps):
        r, a = top[m], aug[m]
        ahead = m + 1 < steps
        v = [across(r, 8 * m + k) for k in range(8)]
        if ahead:
            nr, na = top[m + 1], aug[m + 1]
            w = [across(nr, 8 * m + k) for k in range(8)]
        for j in range(8):
            root = lax.rsqrt(down(v[j], j))
            f = jnp.where(rowid > j, v[j] * root, 0.0)
            yr, ya = down(r, j) * root, down(a, j) * root
            if ahead:
                g = w[j] * root
            for k in range(j + 1, 8):
                q = down(v[k], j) * root
                v[k] = v[k] - f * q
                if ahead:
                    w[k] = w[k] - g * q
            r = jnp.where(rowid == j, yr, r - f * yr)
            a = jnp.where(rowid == j, ya, a - f * ya)
            if ahead:
                nr = nr - g * yr
                na = na - g * ya
        done.append(a)
        if ahead:
            top[m + 1], aug[m + 1] = nr, na
        if m + 2 < steps:
            ra, rb, rc = split3(r)
            aa, ab, ac = split3(a)
            left = jnp.concatenate([ra, ra, rb, ra, rb, rc], axis=0)
            right = jnp.concatenate(
                [
                    jnp.concatenate([x, y], axis=1)
                    for x, y in ((ra, aa), (rb, ab), (ra, aa), (rc, ac), (rb, ab), (ra, aa))
                ],
                axis=0,
            )
            out = lax.dot_general(left, right, TN, preferred_element_type=jnp.float32)
            for i in range(m + 2, steps):
                top[i] = top[i] - out[8 * i : 8 * i + 8, :128]
                aug[i] = aug[i] - out[8 * i : 8 * i + 8, 128:]
        hook(m)
    return jnp.concatenate(done, axis=0)


def factor_inverse(A, N, M, hook):
    for k in range(4):
        rk = slice(128 * k, 128 * k + 128)
        w = base_inverse(A[rk, rk], lambda m, k=k: hook(k, m))
        if k > 0:
            M[rk, :128 * k] = dot3(w, N[rk, :128 * k], (((1,), (0,)), ((), ())))
        M[rk, rk] = w
        if k < 3:
            M[rk, 128 * (k + 1):] = jnp.zeros((128, 512 - 128 * (k + 1)), jnp.float32)
            y = dot3(w, A[rk, 128 * (k + 1):], (((1,), (0,)), ((), ())))
            ym = M[rk, :128 * (k + 1)]
            for i in range(k + 1, 4):
                ri = slice(128 * i, 128 * i + 128)
                yi = y[:, 128 * (i - k - 1):128 * (i - k)]
                A[ri, 128 * i:] = A[ri, 128 * i:] - dot3(yi, y[:, 128 * (i - k - 1):], TN)
                up = dot3(yi, ym, TN)
                if k > 0:
                    N[ri, :128 * k] = N[ri, :128 * k] - up[:, :128 * k]
                N[ri, rk] = -up[:, 128 * k:]


def split2(x):
    a = x.astype(jnp.bfloat16)
    return a, (x - a.astype(jnp.float32)).astype(jnp.bfloat16)


def dot2(x, y, dims):
    xa, xb = split2(x)
    ya, yb = split2(y)

    def one(p, q):
        return lax.dot_general(p, q, dims, preferred_element_type=jnp.float32)

    return one(xa, ya) + (one(xa, yb) + one(xb, ya))


def whole_kernel(
    seed_ref, ridge_ref, grads_hbm, sel_ref, pan, trail,
    grads_ref, T, chosen_ref, cvec_ref, sign_ref, parts, fp, fr, fc, prx, rx, A, N, M, X,
    ps, pr, ms, mr, pys, pyr, mys, myr, rps, rpr, pzs, pzr,
    rs_, rr_, ls_, lr_, ras, rar, rds, rdr, pas, par, pds, pdr, loc, fetched,
):
    z, t, b = lax.axis_index("ex"), lax.axis_index("tp"), lax.axis_index("blk")
    u, c = t // 2, t % 2
    slot = slot_of(b)
    scaling = jnp.float32(1.0 / math.sqrt(GDIM))
    pool, coords = grads_ref.shape
    pending = []

    def to(**axes):
        at = {"ex": z, "tp": t, "blk": b}
        at.update(axes)
        return (at["ex"], at["tp"], at["blk"])

    def copy(src, dst, send, recv, target):
        return pltpu.make_async_remote_copy(
            src_ref=src, dst_ref=dst, send_sem=send, recv_sem=recv,
            device_id=target, device_id_type=pl.DeviceIdType.MESH,
        )

    def go(src, dst, send, recv, target):
        one = copy(src, dst, send, recv, target)
        one.start()
        pending.append(one)
        return one

    def lanes(index):
        return pl.ds(pl.multiple_of(index * SB, SB), SB)

    tp_peers = [(d, lax.rem(t + d, TP)) for d in range(1, TP)]
    chip_peers = [(d, lax.rem(u + d, CHIPS) * 2 + c) for d in range(1, CHIPS)]
    blk_peers = [(d, lax.rem(b + d, BLK)) for d in range(1, BLK)]
    ex_peers = [(d, lax.rem(z + d, EX)) for d in range(1, EX)]
    other = u * 2 + 1 - c
    mate = to(ex=u, tp=2 * z + b // 2, blk=2 * c + b % 2)
    alone = jnp.logical_and(u == z, b // 2 == c)

    barrier = pltpu.get_barrier_semaphore()

    def greet(target):
        pl.semaphore_signal(barrier, inc=1, device_id=target, device_id_type=pl.DeviceIdType.MESH)

    for _, p in tp_peers:
        greet(to(tp=p))
    for _, p in blk_peers:
        greet(to(blk=p))
    for _, p in ex_peers:
        greet(to(ex=p))

    fetch = pltpu.make_async_copy(grads_hbm, grads_ref, fetched)
    fetch.start()
    hot = (lax.broadcasted_iota(jnp.int32, (pool, SB), 0) == sel_ref[...]).astype(jnp.float32)
    hot = hot.astype(jnp.bfloat16)
    cvec_ref[...] = (t * coords + lax.broadcasted_iota(jnp.int32, (8, coords), 1)) * jnp.int32(C1) + seed_ref[0]
    fetch.wait()
    for s in range(coords // 256):
        chosen_ref[pl.ds(s * 256, 256), :] = lax.dot_general(
            grads_ref[:, s * 256 : (s + 1) * 256], hot, TN, preferred_element_type=jnp.float32
        ).astype(jnp.bfloat16)

    def product(block):
        first = block * PANEL + slot * SB

        def rows(r, carry):
            ids = first + r * 16 + lax.broadcasted_iota(jnp.int32, (8, 128), 0)
            low = ids * jnp.int32(C2)
            high = low + jnp.int32(wrap(8 * C2))
            start = pl.multiple_of(r * 16, 16)
            for s in range(coords // 128):
                at = cvec_ref[:, s * 128 : (s + 1) * 128]
                halves = []
                for f in (low, high):
                    h = at + f
                    h = (h ^ right_shift(h, 16)) * jnp.int32(C3)
                    h = (h ^ right_shift(h, 13)) * jnp.int32(C4)
                    h = h ^ (h << 16)
                    halves.append(jnp.where(h < 0, jnp.float32(-1), jnp.float32(1)))
                sign_ref[pl.ds(start, 16), s * 128 : (s + 1) * 128] = jnp.concatenate(halves, axis=0).astype(
                    jnp.bfloat16
                )
            return carry

        lax.fori_loop(0, SB // 16, rows, 0)
        out = jnp.dot(sign_ref[...], chosen_ref[...], preferred_element_type=jnp.float32)
        parts[block] = out.astype(jnp.bfloat16)

    product(0)
    pl.semaphore_wait(barrier, len(tp_peers) + len(blk_peers) + len(ex_peers))

    panel_in = []
    for d, p in tp_peers:
        rows16 = pl.ds(pl.multiple_of((p // 2) * 16, 16), 16)
        panel_in.append(go(parts.at[0, rows16, :], prx.at[d], ps.at[d], pr.at[d], to(tp=p)))

    def share(d):
        p = lax.rem(t + d, TP)
        return copy(parts.at[p], rx.at[d], ms.at[d], mr.at[d], to(tp=p))

    def blocks(lo, hi):
        def body(d, carry):
            p = lax.rem(t + d, TP)

            @pl.when(p != 0)
            def _():
                product(p)

            share(d).start()
            return carry

        lax.fori_loop(lo, hi, body, 0)

    blocks(1, CUT1)
    for one in panel_in:
        one.wait_recv()
    total = parts[0, pl.ds(pl.multiple_of(u * 16, 16), 16), :].astype(jnp.float32)
    for d in range(1, TP):
        total = total + prx[d].astype(jnp.float32)
    fp[slot, u, :, lanes(z)] = (total * scaling).astype(jnp.bfloat16)
    mine = fp.at[slot, u, :, lanes(z)]
    panel_y = [go(mine, mine, pys.at[d], pyr.at[d], to(blk=p)) for d, p in blk_peers]

    blocks(CUT1, CUT2)
    for one in panel_y:
        one.wait_recv()
    mine = fp.at[:, u, :, lanes(z)]
    panel_z = [go(mine, mine, pzs.at[d], pzr.at[d], to(ex=p)) for d, p in ex_peers]

    blocks(CUT2, TP)

    @pl.when(t != 0)
    def _():
        product(t)

    for one in panel_z:
        one.wait_recv()

    def panel_at(chip, half):
        return fp.at[2 * c + half, chip]

    panel_a = []
    for half in range(2):
        mine = panel_at(u, half)
        for d, p in chip_peers:
            k = half * CHIPS + d
            panel_a.append(go(mine, mine, pas.at[k], par.at[k], to(tp=p)))

    for d in range(1, TP):
        share(d).wait_recv()
    total = parts[t].astype(jnp.float32)
    for d in range(1, TP):
        total = total + rx[d].astype(jnp.float32)
    fc[lanes(slot), lanes(z)] = (total * scaling).astype(jnp.bfloat16)
    mine = fc.at[lanes(slot), lanes(z)]
    main_y = [None] + [go(mine, mine, mys.at[d], myr.at[d], to(blk=p)) for d, p in blk_peers]

    row_slot = fr.at[lanes(b // 2), lanes(z)]
    moved = copy(mine, row_slot, rps, rpr, mate)

    right, left = to(ex=lax.rem(z + 1, EX)), to(ex=lax.rem(z + EX - 1, EX))
    rights, lefts = {}, {}

    def piece(step, j):
        row = slot_of(lax.rem(b + BLK - j, BLK))
        return fc.at[lanes(row), lanes(lax.rem(z + step + EX, EX))]

    def pass_right(s, j):
        at = piece(-s, j)
        rights[s, j] = go(at, at, rs_.at[s, j], rr_.at[s, j], right)

    def pass_left(s, j):
        at = piece(s, j)
        lefts[s, j] = go(at, at, ls_.at[s, j], lr_.at[s, j], left)

    pass_right(0, 0)
    pass_left(0, 0)

    def along_blk():
        for j in range(1, BLK):
            main_y[j].wait_recv()
            pass_right(0, j)
            pass_left(0, j)

    def row_at(chip):
        return fr.at[lanes(c), lanes(chip)]

    rows_in, rows_over = [], []

    def rows_out():
        @pl.when(alone)
        def _():
            pltpu.make_async_copy(piece(0, 0), row_slot, loc).wait()

        @pl.when(jnp.logical_not(alone))
        def _():
            moved.wait_send()
            moved.wait_recv()

        mine = row_at(u)
        rows_in.extend(go(mine, mine, ras.at[d], rar.at[d], to(tp=p)) for d, p in chip_peers)
        rows_over.append(go(mine, mine, rds.at[0], rdr.at[0], to(tp=other)))

    def ring(s, js):
        for j in js:
            rights[s - 1, j].wait_recv()
            if s < EX // 2 - 1 or j < BLK // 2:
                pass_right(s, j)
            lefts[s - 1, j].wait_recv()
            if s < EX // 2 - 1 or j >= BLK // 2:
                pass_left(s, j)

    def rows_across():
        for d in range(1, CHIPS):
            rows_in[d - 1].wait_recv()
            at = row_at(lax.rem(u + CHIPS - d, CHIPS))
            rows_over.append(go(at, at, rds.at[d], rdr.at[d], to(tp=other)))

    along_blk()
    ring(1, (0,))

    panel_over = []

    def panel_across(half):
        for d in range(1, CHIPS):
            panel_a[half * (CHIPS - 1) + d - 1].wait_recv()
            at = panel_at(lax.rem(u + CHIPS - d, CHIPS), half)
            k = half * CHIPS + d
            panel_over.append(go(at, at, pds.at[k], pdr.at[k], to(tp=other)))

    def panel_done(half):
        for one in panel_over[half * (CHIPS - 1) :]:
            one.wait_recv()

    panel_across(0)
    panel_done(0)

    @pl.when(alone)
    def _():
        pltpu.make_async_copy(piece(0, 0), row_slot, loc).start()

    @pl.when(jnp.logical_not(alone))
    def _():
        moved.start()

    def columns_here():
        last = EX // 2 - 1
        for j in range(BLK // 2):
            rights[last, j].wait_recv()
            lefts[last, BLK // 2 + j].wait_recv()
        T[...] = gram(fp[...].reshape(PANEL, EXAMPLES), fc[...], 0, t * PANEL)

    def panel_here():
        panel_done(1)
        panel = fp[...].reshape(PANEL, EXAMPLES)
        A[...] = gram(panel, panel, 0, 0)

    actions = {
        (0, 3): (lambda: ring(1, (1,)),),
        (0, 7): (lambda: ring(1, (2,)),),
        (0, 11): (lambda: ring(1, (3,)),),
        (0, 12): (lambda: panel_across(1),),
        (0, 15): (panel_here,),
        (1, 0): (lambda: ring(2, (0,)),),
        (1, 3): (lambda: ring(2, (1,)),),
        (1, 6): (lambda: ring(2, (2,)),),
        (1, 8): (rows_out,),
        (1, 9): (lambda: ring(2, (3,)),),
        (1, 14): (lambda: ring(3, (0,)),),
        (2, 2): (lambda: ring(3, (1,)),),
        (2, 5): (lambda: ring(3, (2,)),),
        (2, 8): (lambda: ring(3, (3,)),),
        (3, 1): (columns_here,),
        (3, 6): (rows_across,),
    }

    def hook(k, m):
        for act in actions.get((k, m), ()):
            act()

    g = z * BLK + b
    inv = jnp.float32(1.0 / EXAMPLES)
    rv = ridge_ref[0]

    def gram(left_part, right_part, r0, c0):
        out = lax.dot_general(left_part, right_part, NT, preferred_element_type=jnp.float32) * inv
        rows_, cols_ = (lax.broadcasted_iota(jnp.int32, out.shape, k) for k in range(2))
        return out + jnp.where(rows_ + r0 == cols_ + c0, rv, 0.0)

    corner = fp[0].reshape(SB, EXAMPLES)
    A[:SB, :SB] = gram(corner, corner, 0, 0)
    factor_inverse(A, N, M, hook)

    for one in rows_over:
        one.wait_recv()
    for one in pending:
        one.wait_send()
    for d in range(1, TP):
        share(d).wait_send()

    panel = fp[...].reshape(PANEL, EXAMPLES)
    X[...] = dot2(M[...], T[...], NN)
    first_tile = gram(fr[...], panel, g * 2 * SB, 0)
    own = gram(fr[...], fc[...], g * 2 * SB, t * PANEL)
    out = dot2(first_tile, M[...], NT)
    pan[...] = out
    trail[...] = own - dot2(out, X[...], NN)


def whole(seed, ridge, grads, sel):
    bf, f32 = jnp.bfloat16, jnp.float32
    coords = grads.shape[1]
    dma = pltpu.SemaphoreType.DMA
    sems = []
    for n in (TP, TP, BLK, BLK):
        sems += [dma((n,)), dma((n,))]
    sems += [dma, dma, dma((EX,)), dma((EX,))]
    sems += [dma((EX // 2, BLK))] * 4
    sems += [dma((CHIPS,))] * 4 + [dma((2 * CHIPS,))] * 4
    sems += [dma, dma]
    vmem = pl.BlockSpec(memory_space=pltpu.VMEM)
    smem = pl.BlockSpec(memory_space=pltpu.SMEM)
    tile = jax.ShapeDtypeStruct((2 * SB, PANEL), f32)
    square = pltpu.VMEM((PANEL, PANEL), f32)
    return pl.pallas_call(
        whole_kernel,
        out_shape=(tile, tile),
        in_specs=[smem, smem, pl.BlockSpec(memory_space=pl.ANY), vmem],
        out_specs=(vmem, vmem),
        scratch_shapes=[
            pltpu.VMEM(grads.shape, bf),
            square,
            pltpu.VMEM((coords, SB), bf),
            pltpu.VMEM((8, coords), jnp.int32),
            pltpu.VMEM((SB, coords), bf),
            pltpu.VMEM((TP, SB, SB), bf),
            pltpu.VMEM((BLK, CHIPS, 16, EXAMPLES), bf),
            pltpu.VMEM((2 * SB, EXAMPLES), bf),
            pltpu.VMEM((PANEL, EXAMPLES), bf),
            pltpu.VMEM((TP, 16, SB), bf),
            pltpu.VMEM((TP, SB, SB), bf),
            square, square, square, square,
            *sems,
        ],
        compiler_params=pltpu.CompilerParams(collective_id=0, has_side_effects=True),
        name="whole",
    )(seed, ridge, grads, sel)


def shards(gradients, selection, seed_value, ridge_value):
    return whole(seed_value, ridge_value, gradients, selection.reshape(1, SB))


def solution(mesh):
    in_specs = (P("ex", "tp"), P("ex"), P(), P())
    out_specs = (P(("ex", "blk"), None), P(("ex", "blk"), "tp"))
    return jax.shard_map(shards, mesh=mesh, in_specs=in_specs, out_specs=out_specs, check_vma=False)
```

```python
import math

import jax
import jax.numpy as jnp
from jax import lax
from jax.experimental import pallas as pl
from jax.experimental.pallas import tpu as pltpu
from jax.sharding import PartitionSpec as P

SB = 128
EX, TP, BLK = 8, 16, 4
CHIPS = TP // 2
K, GDIM, EXAMPLES, PANEL = 8192, 32768, 1024, 512
HI = lax.Precision.HIGHEST
NT = (((1,), (1,)), ((), ()))
TN = (((0,), (0,)), ((), ()))
NN = (((1,), (0,)), ((), ()))


def wrap(value):
    value &= 0xFFFFFFFF
    return value - (1 << 32) if value >= (1 << 31) else value


C1, C2, C3 = -1640531535, 668265263, -2048144789
CUT1, CUT2 = 6, 11
C4 = wrap(-1028477387 << 8)


def slot_of(b):
    return 2 * (b % 2) + b // 2


def right_shift(value, amount):
    return lax.shift_right_logical(value, jnp.full_like(value, amount))


def split3(x):
    a = x.astype(jnp.bfloat16)
    r = x - a.astype(jnp.float32)
    b = r.astype(jnp.bfloat16)
    c = (r - b.astype(jnp.float32)).astype(jnp.bfloat16)
    return a, b, c

def dot3(x, y, dims):
    xa, xb, xc = split3(x)
    ya, yb, yc = split3(y)
    kx, ky = dims[0][0][0], dims[0][1][0]
    left = jnp.concatenate([xa, xa, xb, xa, xb, xc], axis=kx)
    right = jnp.concatenate([ya, yb, ya, yc, yb, ya], axis=ky)
    return lax.dot_general(left, right, dims, preferred_element_type=jnp.float32)

def base_inverse(s, hook):
    n = 128
    steps = n // 8
    rowid = lax.broadcasted_iota(jnp.int32, (8, 128), 0)
    lane = lax.broadcasted_iota(jnp.int32, (8, 128), 1)
    top = [s[8 * i : 8 * i + 8, :] for i in range(steps)]
    aug = [(lane == rowid + 8 * i).astype(jnp.float32) for i in range(steps)]

    def across(x, k):
        return jnp.broadcast_to(x[:, k : k + 1], (8, 128))

    def down(x, j):
        return jnp.broadcast_to(x[j : j + 1, :], (8, 128))

    done = []
    for m in range(steps):
        r, a = top[m], aug[m]
        ahead = m + 1 < steps
        v = [across(r, 8 * m + k) for k in range(8)]
        if ahead:
            nr, na = top[m + 1], aug[m + 1]
            w = [across(nr, 8 * m + k) for k in range(8)]
        for j in range(8):
            root = lax.rsqrt(down(v[j], j))
            f = jnp.where(rowid > j, v[j] * root, 0.0)
            yr, ya = down(r, j) * root, down(a, j) * root
            if ahead:
                g = w[j] * root
            for k in range(j + 1, 8):
                q = down(v[k], j) * root
                v[k] = v[k] - f * q
                if ahead:
                    w[k] = w[k] - g * q
            r = jnp.where(rowid == j, yr, r - f * yr)
            a = jnp.where(rowid == j, ya, a - f * ya)
            if ahead:
                nr = nr - g * yr
                na = na - g * ya
        done.append(a)
        if ahead:
            top[m + 1], aug[m + 1] = nr, na
        if m + 2 < steps:
            ra, rb, rc = split3(r)
            aa, ab, ac = split3(a)
            left = jnp.concatenate([ra, ra, rb, ra, rb, rc], axis=0)
            right = jnp.concatenate(
                [
                    jnp.concatenate([x, y], axis=1)
                    for x, y in ((ra, aa), (rb, ab), (ra, aa), (rc, ac), (rb, ab), (ra, aa))
                ],
                axis=0,
            )
            out = lax.dot_general(left, right, TN, preferred_element_type=jnp.float32)
            for i in range(m + 2, steps):
                top[i] = top[i] - out[8 * i : 8 * i + 8, :128]
                aug[i] = aug[i] - out[8 * i : 8 * i + 8, 128:]
        hook(m)
    return jnp.concatenate(done, axis=0)


def factor_inverse(A, N, M, hook):
    for k in range(4):
        rk = slice(128 * k, 128 * k + 128)
        w = base_inverse(A[rk, rk], lambda m, k=k: hook(k, m))
        if k > 0:
            M[rk, :128 * k] = dot3(w, N[rk, :128 * k], (((1,), (0,)), ((), ())))
        M[rk, rk] = w
        if k < 3:
            M[rk, 128 * (k + 1):] = jnp.zeros((128, 512 - 128 * (k + 1)), jnp.float32)
            y = dot3(w, A[rk, 128 * (k + 1):], (((1,), (0,)), ((), ())))
            ym = M[rk, :128 * (k + 1)]
            for i in range(k + 1, 4):
                ri = slice(128 * i, 128 * i + 128)
                yi = y[:, 128 * (i - k - 1):128 * (i - k)]
                A[ri, 128 * i:] = A[ri, 128 * i:] - dot3(yi, y[:, 128 * (i - k - 1):], TN)
                up = dot3(yi, ym, TN)
                if k > 0:
                    N[ri, :128 * k] = N[ri, :128 * k] - up[:, :128 * k]
                N[ri, rk] = -up[:, 128 * k:]


def split2(x):
    a = x.astype(jnp.bfloat16)
    return a, (x - a.astype(jnp.float32)).astype(jnp.bfloat16)


def dot2(x, y, dims):
    xa, xb = split2(x)
    ya, yb = split2(y)

    def one(p, q):
        return lax.dot_general(p, q, dims, preferred_element_type=jnp.float32)

    return one(xa, ya) + (one(xa, yb) + one(xb, ya))


def whole_kernel(
    seed_ref, ridge_ref, grads_hbm, sel_ref, pan, trail,
    grads_ref, T, chosen_ref, cvec_ref, sign_ref, parts, fp, fr, fc, prx, rx, A, N, M, X,
    ps, pr, ms, mr, pys, pyr, mys, myr, rps, rpr, pzs, pzr,
    rs_, rr_, ls_, lr_, ras, rar, rds, rdr, pas, par, pds, pdr, loc, fetched,
):
    z, t, b = lax.axis_index("ex"), lax.axis_index("tp"), lax.axis_index("blk")
    u, c = t // 2, t % 2
    slot = slot_of(b)
    scaling = jnp.float32(1.0 / math.sqrt(GDIM))
    pool, coords = grads_ref.shape
    pending = []

    def to(**axes):
        at = {"ex": z, "tp": t, "blk": b}
        at.update(axes)
        return (at["ex"], at["tp"], at["blk"])

    def copy(src, dst, send, recv, target):
        return pltpu.make_async_remote_copy(
            src_ref=src, dst_ref=dst, send_sem=send, recv_sem=recv,
            device_id=target, device_id_type=pl.DeviceIdType.MESH,
        )

    def go(src, dst, send, recv, target):
        one = copy(src, dst, send, recv, target)
        one.start()
        pending.append(one)
        return one

    def lanes(index):
        return pl.ds(pl.multiple_of(index * SB, SB), SB)

    tp_peers = [(d, lax.rem(t + d, TP)) for d in range(1, TP)]
    chip_peers = [(d, lax.rem(u + d, CHIPS) * 2 + c) for d in range(1, CHIPS)]
    blk_peers = [(d, lax.rem(b + d, BLK)) for d in range(1, BLK)]
    ex_peers = [(d, lax.rem(z + d, EX)) for d in range(1, EX)]
    other = u * 2 + 1 - c
    mate = to(ex=u, tp=2 * z + b // 2, blk=2 * c + b % 2)
    alone = jnp.logical_and(u == z, b // 2 == c)

    barrier = pltpu.get_barrier_semaphore()

    def greet(target):
        pl.semaphore_signal(barrier, inc=1, device_id=target, device_id_type=pl.DeviceIdType.MESH)

    for _, p in tp_peers:
        greet(to(tp=p))
    for _, p in blk_peers:
        greet(to(blk=p))
    for _, p in ex_peers:
        greet(to(ex=p))

    fetch = pltpu.make_async_copy(grads_hbm, grads_ref, fetched)
    fetch.start()
    hot = (lax.broadcasted_iota(jnp.int32, (pool, SB), 0) == sel_ref[...]).astype(jnp.float32)
    hot = hot.astype(jnp.bfloat16)
    cvec_ref[...] = (t * coords + lax.broadcasted_iota(jnp.int32, (8, coords), 1)) * jnp.int32(C1) + seed_ref[0]
    fetch.wait()
    for s in range(coords // 256):
        chosen_ref[pl.ds(s * 256, 256), :] = lax.dot_general(
            grads_ref[:, s * 256 : (s + 1) * 256], hot, TN, preferred_element_type=jnp.float32
        ).astype(jnp.bfloat16)

    def product(block):
        first = block * PANEL + slot * SB

        def rows(r, carry):
            ids = first + r * 16 + lax.broadcasted_iota(jnp.int32, (8, 128), 0)
            low = ids * jnp.int32(C2)
            high = low + jnp.int32(wrap(8 * C2))
            start = pl.multiple_of(r * 16, 16)
            for s in range(coords // 128):
                at = cvec_ref[:, s * 128 : (s + 1) * 128]
                halves = []
                for f in (low, high):
                    h = at + f
                    h = (h ^ right_shift(h, 16)) * jnp.int32(C3)
                    h = (h ^ right_shift(h, 13)) * jnp.int32(C4)
                    h = h ^ (h << 16)
                    halves.append(jnp.where(h < 0, jnp.float32(-1), jnp.float32(1)))
                sign_ref[pl.ds(start, 16), s * 128 : (s + 1) * 128] = jnp.concatenate(halves, axis=0).astype(
                    jnp.bfloat16
                )
            return carry

        lax.fori_loop(0, SB // 16, rows, 0)
        out = jnp.dot(sign_ref[...], chosen_ref[...], preferred_element_type=jnp.float32)
        parts[block] = out.astype(jnp.bfloat16)

    product(0)
    pl.semaphore_wait(barrier, len(tp_peers) + len(blk_peers) + len(ex_peers))

    panel_in = []
    for d, p in tp_peers:
        rows16 = pl.ds(pl.multiple_of((p // 2) * 16, 16), 16)
        panel_in.append(go(parts.at[0, rows16, :], prx.at[d], ps.at[d], pr.at[d], to(tp=p)))

    def share(d):
        p = lax.rem(t + d, TP)
        return copy(parts.at[p], rx.at[d], ms.at[d], mr.at[d], to(tp=p))

    def blocks(lo, hi):
        def body(d, carry):
            p = lax.rem(t + d, TP)

            @pl.when(p != 0)
            def _():
                product(p)

            share(d).start()
            return carry

        lax.fori_loop(lo, hi, body, 0)

    blocks(1, CUT1)
    for one in panel_in:
        one.wait_recv()
    total = parts[0, pl.ds(pl.multiple_of(u * 16, 16), 16), :].astype(jnp.float32)
    for d in range(1, TP):
        total = total + prx[d].astype(jnp.float32)
    fp[slot, u, :, lanes(z)] = (total * scaling).astype(jnp.bfloat16)
    mine = fp.at[slot, u, :, lanes(z)]
    panel_y = [go(mine, mine, pys.at[d], pyr.at[d], to(blk=p)) for d, p in blk_peers]

    blocks(CUT1, CUT2)
    for one in panel_y:
        one.wait_recv()
    mine = fp.at[:, u, :, lanes(z)]
    panel_z = [go(mine, mine, pzs.at[d], pzr.at[d], to(ex=p)) for d, p in ex_peers]

    blocks(CUT2, TP)

    @pl.when(t != 0)
    def _():
        product(t)

    for one in panel_z:
        one.wait_recv()

    def panel_at(chip):
        return fp.at[pl.ds(2 * c, 2), chip]

    mine = panel_at(u)
    panel_a = [go(mine, mine, pas.at[d], par.at[d], to(tp=p)) for d, p in chip_peers]

    for d in range(1, TP):
        share(d).wait_recv()
    total = parts[t].astype(jnp.float32)
    for d in range(1, TP):
        total = total + rx[d].astype(jnp.float32)
    fc[lanes(slot), lanes(z)] = (total * scaling).astype(jnp.bfloat16)
    mine = fc.at[lanes(slot), lanes(z)]
    main_y = [None] + [go(mine, mine, mys.at[d], myr.at[d], to(blk=p)) for d, p in blk_peers]

    row_slot = fr.at[lanes(b // 2), lanes(z)]
    moved = copy(mine, row_slot, rps, rpr, mate)

    right, left = to(ex=lax.rem(z + 1, EX)), to(ex=lax.rem(z + EX - 1, EX))
    rights, lefts = {}, {}

    def piece(step, j):
        row = slot_of(lax.rem(b + BLK - j, BLK))
        return fc.at[lanes(row), lanes(lax.rem(z + step + EX, EX))]

    def pass_right(s, j):
        at = piece(-s, j)
        rights[s, j] = go(at, at, rs_.at[s, j], rr_.at[s, j], right)

    def pass_left(s, j):
        at = piece(s, j)
        lefts[s, j] = go(at, at, ls_.at[s, j], lr_.at[s, j], left)

    pass_right(0, 0)
    pass_left(0, 0)

    def along_blk():
        for j in range(1, BLK):
            main_y[j].wait_recv()
            pass_right(0, j)
            pass_left(0, j)

    def row_at(chip):
        return fr.at[lanes(c), lanes(chip)]

    rows_in, rows_over = [], []

    def rows_out():
        @pl.when(alone)
        def _():
            pltpu.make_async_copy(piece(0, 0), row_slot, loc).wait()

        @pl.when(jnp.logical_not(alone))
        def _():
            moved.wait_send()
            moved.wait_recv()

        mine = row_at(u)
        rows_in.extend(go(mine, mine, ras.at[d], rar.at[d], to(tp=p)) for d, p in chip_peers)
        rows_over.append(go(mine, mine, rds.at[0], rdr.at[0], to(tp=other)))

    def ring(s, js):
        for j in js:
            rights[s - 1, j].wait_recv()
            if s < EX // 2 - 1 or j < BLK // 2:
                pass_right(s, j)
            lefts[s - 1, j].wait_recv()
            if s < EX // 2 - 1 or j >= BLK // 2:
                pass_left(s, j)

    def rows_across():
        for d in range(1, CHIPS):
            rows_in[d - 1].wait_recv()
            at = row_at(lax.rem(u + CHIPS - d, CHIPS))
            rows_over.append(go(at, at, rds.at[d], rdr.at[d], to(tp=other)))

    panel_over = []
    for d in range(1, CHIPS):
        panel_a[d - 1].wait_recv()
        at = panel_at(lax.rem(u + CHIPS - d, CHIPS))
        panel_over.append(go(at, at, pds.at[d], pdr.at[d], to(tp=other)))
    along_blk()
    ring(1, (0,))
    for one in panel_over:
        one.wait_recv()

    @pl.when(alone)
    def _():
        pltpu.make_async_copy(piece(0, 0), row_slot, loc).start()

    @pl.when(jnp.logical_not(alone))
    def _():
        moved.start()

    def columns_here():
        last = EX // 2 - 1
        for j in range(BLK // 2):
            rights[last, j].wait_recv()
            lefts[last, BLK // 2 + j].wait_recv()
        T[...] = gram(fp[...].reshape(PANEL, EXAMPLES), fc[...], 0, t * PANEL)

    actions = {
        (0, 3): (lambda: ring(1, (1,)),),
        (0, 7): (lambda: ring(1, (2,)),),
        (0, 11): (lambda: ring(1, (3,)),),
        (1, 0): (lambda: ring(2, (0,)),),
        (1, 3): (lambda: ring(2, (1,)),),
        (1, 6): (lambda: ring(2, (2,)),),
        (1, 8): (rows_out,),
        (1, 9): (lambda: ring(2, (3,)),),
        (1, 14): (lambda: ring(3, (0,)),),
        (2, 2): (lambda: ring(3, (1,)),),
        (2, 5): (lambda: ring(3, (2,)),),
        (2, 8): (lambda: ring(3, (3,)),),
        (3, 1): (columns_here,),
        (3, 6): (rows_across,),
    }

    def hook(k, m):
        for act in actions.get((k, m), ()):
            act()

    g = z * BLK + b
    inv = jnp.float32(1.0 / EXAMPLES)
    rv = ridge_ref[0]

    def gram(left_part, right_part, r0, c0):
        out = lax.dot_general(left_part, right_part, NT, preferred_element_type=jnp.float32) * inv
        rows_, cols_ = (lax.broadcasted_iota(jnp.int32, out.shape, k) for k in range(2))
        return out + jnp.where(rows_ + r0 == cols_ + c0, rv, 0.0)

    panel = fp[...].reshape(PANEL, EXAMPLES)
    A[...] = gram(panel, panel, 0, 0)
    factor_inverse(A, N, M, hook)

    for one in rows_over:
        one.wait_recv()
    for one in pending:
        one.wait_send()
    for d in range(1, TP):
        share(d).wait_send()

    panel = fp[...].reshape(PANEL, EXAMPLES)
    X[...] = dot2(M[...], T[...], NN)
    first_tile = gram(fr[...], panel, g * 2 * SB, 0)
    own = gram(fr[...], fc[...], g * 2 * SB, t * PANEL)
    out = dot2(first_tile, M[...], NT)
    pan[...] = out
    trail[...] = own - dot2(out, X[...], NN)


def whole(seed, ridge, grads, sel):
    bf, f32 = jnp.bfloat16, jnp.float32
    coords = grads.shape[1]
    dma = pltpu.SemaphoreType.DMA
    sems = []
    for n in (TP, TP, BLK, BLK):
        sems += [dma((n,)), dma((n,))]
    sems += [dma, dma, dma((EX,)), dma((EX,))]
    sems += [dma((EX // 2, BLK))] * 4
    sems += [dma((CHIPS,))] * 8
    sems += [dma, dma]
    vmem = pl.BlockSpec(memory_space=pltpu.VMEM)
    smem = pl.BlockSpec(memory_space=pltpu.SMEM)
    tile = jax.ShapeDtypeStruct((2 * SB, PANEL), f32)
    square = pltpu.VMEM((PANEL, PANEL), f32)
    return pl.pallas_call(
        whole_kernel,
        out_shape=(tile, tile),
        in_specs=[smem, smem, pl.BlockSpec(memory_space=pl.ANY), vmem],
        out_specs=(vmem, vmem),
        scratch_shapes=[
            pltpu.VMEM(grads.shape, bf),
            square,
            pltpu.VMEM((coords, SB), bf),
            pltpu.VMEM((8, coords), jnp.int32),
            pltpu.VMEM((SB, coords), bf),
            pltpu.VMEM((TP, SB, SB), bf),
            pltpu.VMEM((BLK, CHIPS, 16, EXAMPLES), bf),
            pltpu.VMEM((2 * SB, EXAMPLES), bf),
            pltpu.VMEM((PANEL, EXAMPLES), bf),
            pltpu.VMEM((TP, 16, SB), bf),
            pltpu.VMEM((TP, SB, SB), bf),
            square, square, square, square,
            *sems,
        ],
        compiler_params=pltpu.CompilerParams(collective_id=0, has_side_effects=True),
        name="whole",
    )(seed, ridge, grads, sel)


def shards(gradients, selection, seed_value, ridge_value):
    return whole(seed_value, ridge_value, gradients, selection.reshape(1, SB))


def solution(mesh):
    in_specs = (P("ex", "tp"), P("ex"), P(), P())
    out_specs = (P(("ex", "blk"), None), P(("ex", "blk"), "tp"))
    return jax.shard_map(shards, mesh=mesh, in_specs=in_specs, out_specs=out_specs, check_vma=False)
```
